128 devices in a mesh: seq: 16 (over y, z_hi, core), head: 8 (over x, z_lo).
Axes of the slice: x: 4, y: 4, z: 4 (z_hi: 2, z_lo: 2; z = z_hi * 2 + z_lo), core: 2. Of those that a mesh axis runs over, the one named last changes fastest.
Arguments:
- teacher_queries: bfloat16 [4096, 8192], P('seq', 'head'), may hold values from -16 to 16, as said below
- student_queries: bfloat16 [4096, 4096], P('seq', 'head'), may hold values from -16 to 16, as said below
- token_counts: int32 [16], replicated, may hold values from 1 to 256, 3072 in all
Outputs:
- student_grad: float32 [4096, 4096], P('seq', 'head')
- loss: float32 [], replicated
The draws below stay inside these ranges and needn't reach their ends.
Inputs may be any that keep to these rules, and one draw needn't show every extreme that they name: `teacher_queries`: query entries are real values of order one; the entries of a row may share a scale. `student_queries`: query entries are real values of order one; the entries of a row may share a scale. `token_counts`: the counts sum to 3072; the largest equals 256.
All inputs are finite; a program needn't handle non-finite values.
Results may differ from the reference program's by a relative error of at most 0.0035.
Values may be sent and summed in bfloat16 or wider, within the bound.
A program may use at most 64 MiB of HBM per device.

```python
import math
import jax
import jax.numpy as jnp
import numpy as np
from jax import lax

DT = 8192
DS = 4096
H_REL = 128
TOK_DEV = 256
SEQ_LEN = 4096
LIVE = 3072
N_SEQ = 16


def draw_teacher_queries(key, part):
    values = jax.random.normal(key, (SEQ_LEN, DT), jnp.float32)
    return jnp.clip(values, -16.0, 16.0).astype(jnp.bfloat16)


def draw_student_queries(key, part):
    values = jax.random.normal(key, (SEQ_LEN, DS), jnp.float32)
    return jnp.clip(values, -16.0, 16.0).astype(jnp.bfloat16)


def length_profile(count, total, most, skew):
    loads = [(1 << 20) // math.isqrt(standing ** skew) + 1 for standing in range(2, count + 1)]
    surplus, given = total - most - (count - 1), [1] * (count - 1)
    while surplus > 0:
        candidates = [i for i in range(count - 1) if given[i] < most]
        mass, budget = sum([loads[i] for i in candidates]), surplus
        for i in candidates:
            addition = min(most - given[i], max(1, budget * loads[i] // mass), surplus)
            given[i] = given[i] + addition
            surplus = surplus - addition
    return np.array([most] + given)


def uneven(key, count, total, bound, slope):
    if count == 2:
        one = jax.random.randint(key, (), max(1, total - bound), min(bound, total - 1) + 1)
        return jnp.stack([one, total - one])
    tallies = jnp.asarray(length_profile(count, total, bound, slope), jnp.int32)
    twos = (count - 1) // 2
    giver, receiver = tallies[1:1 + 2 * twos:2], tallies[2:2 + 2 * twos:2]
    slack = jnp.minimum(giver - 1, bound - receiver)
    moved = jax.random.randint(jax.random.fold_in(key, 1), (twos,), 0, 1 << 20) % (slack + 1)
    tallies = tallies.at[1:1 + 2 * twos:2].set(giver - moved).at[2:2 + 2 * twos:2].set(receiver + moved)
    return tallies[jax.random.permutation(jax.random.fold_in(key, 2), count)]


def setup_inputs(seed: int = 0) -> dict:
    keys = jax.random.split(jax.random.key(seed), 4)
    return {
        "teacher_queries": draw_teacher_queries(jax.random.fold_in(keys[3], 71), 0),
        "student_queries": draw_student_queries(jax.random.fold_in(keys[3], 71), 0),
        "token_counts": uneven(keys[2], N_SEQ, LIVE, TOK_DEV, 2).astype(jnp.int32),
    }


NEGATIVE = -1.0e30


def reference(teacher_queries, student_queries, token_counts):
    seq_rows = SEQ_LEN
    teacher_dim = DT // H_REL
    student_dim = DS // H_REL
    teacher_scale = teacher_dim ** -0.5
    student_scale = student_dim ** -0.5
    positions = jnp.arange(seq_rows, dtype=jnp.int32)
    owner_table = (positions // TOK_DEV)[:, None] == jnp.arange(N_SEQ, dtype=jnp.int32)[None, :]
    real_count = jnp.sum(jnp.where(owner_table, token_counts[None, :], 0), axis=1).astype(jnp.int32)
    is_real = (positions % TOK_DEV) < real_count
    allowed = (positions[None, :] <= positions[:, None]) & (is_real[None, :] | (positions[None, :] == positions[:, None]))
    teacher_heads = teacher_queries.reshape(seq_rows, H_REL, teacher_dim).transpose(1, 0, 2)
    student_heads = student_queries.reshape(seq_rows, H_REL, student_dim).transpose(1, 0, 2)

    def log_probs(logits):
        top_value = jnp.max(jnp.where(allowed, logits, NEGATIVE), axis=1)
        total_sum = jnp.sum(jnp.where(allowed, jnp.exp(logits - top_value[:, None]), 0.0), axis=1)
        return top_value + jnp.log(total_sum)

    def per_head(pair):
        teacher_part = pair[0].astype(jnp.float32)
        student_part = pair[1].astype(jnp.float32)
        teacher_logits = jnp.dot(teacher_part, teacher_part.T, precision=lax.Precision.HIGHEST) * teacher_scale
        student_logits = jnp.dot(student_part, student_part.T, precision=lax.Precision.HIGHEST) * student_scale
        teacher_lse = log_probs(teacher_logits)
        student_lse = log_probs(student_logits)
        teacher_prob = jnp.where(allowed, jnp.exp(teacher_logits - teacher_lse[:, None]), 0.0)
        student_prob = jnp.where(allowed, jnp.exp(student_logits - student_lse[:, None]), 0.0)
        row_kl = jnp.sum(teacher_prob * (teacher_logits - student_logits), axis=1) - teacher_lse + student_lse
        kl_sum = jnp.sum(jnp.where(is_real, row_kl, 0.0))
        weights = jnp.where(is_real[:, None], student_prob - teacher_prob, 0.0).astype(jnp.bfloat16)
        weights = lax.optimization_barrier(weights).astype(jnp.float32)
        gradient = jnp.dot(weights, student_part, precision=lax.Precision.HIGHEST)
        gradient = gradient + jnp.dot(weights.T, student_part, precision=lax.Precision.HIGHEST)
        return kl_sum, gradient * student_scale

    kl_sums, gradients = lax.map(per_head, (teacher_heads, student_heads))
    loss = jnp.sum(kl_sums) / (H_REL * jnp.sum(token_counts).astype(jnp.float32))
    student_grad = gradients.transpose(1, 0, 2).reshape(seq_rows, DS)
    return student_grad, loss
```

```python
import functools

import jax
import jax.numpy as jnp
from jax import lax
from jax.experimental import pallas as pl
from jax.experimental.pallas import tpu as pltpu
from jax.sharding import PartitionSpec as P

H_REL = 128
LIVE = 3072
TILE = 256
LANES = 128
LOG2E = 1.4426950408889634
LN2 = 0.6931471805599453
NEGATIVE = -1e30
MESH = pl.DeviceIdType.MESH
F32 = jnp.float32
BF16 = jnp.bfloat16


def greet(peers):
    barrier = pltpu.get_barrier_semaphore()
    for peer in peers:
        pl.semaphore_signal(barrier, inc=1, device_id=peer, device_id_type=MESH)
    pl.semaphore_wait(barrier, len(peers))


def others(axis, n):
    me = lax.axis_index(axis)
    return me, [lax.rem(me + k, n) for k in range(1, n)]


def send(src, dst, send_sem, recv_sem, device):
    copy = pltpu.make_async_remote_copy(
        src_ref=src, dst_ref=dst, send_sem=send_sem, recv_sem=recv_sem,
        device_id=device, device_id_type=MESH,
    )
    copy.start()
    return copy


def exchange_kernel(n, x_ref, r_ref, send_sem, recv_sem, own_sem):
    me, peers = others("seq", n)
    own = pltpu.make_async_copy(x_ref.at[me], r_ref.at[me], own_sem)
    own.start()
    greet([{"seq": p} for p in peers])
    copies = [
        send(x_ref.at[p], r_ref.at[me], send_sem.at[k], recv_sem.at[k], {"seq": p})
        for k, p in enumerate(peers)
    ]
    own.wait()
    for copy in copies:
        copy.wait()


def exchange(x, n):
    any_space = pl.BlockSpec(memory_space=pl.ANY)
    return pl.pallas_call(
        functools.partial(exchange_kernel, n),
        out_shape=jax.ShapeDtypeStruct(x.shape, x.dtype),
        in_specs=[any_space],
        out_specs=any_space,
        scratch_shapes=[
            pltpu.SemaphoreType.DMA((n - 1,)),
            pltpu.SemaphoreType.DMA((n - 1,)),
            pltpu.SemaphoreType.DMA,
        ],
        compiler_params=pltpu.CompilerParams(collective_id=0, has_side_effects=True),
    )(x)


def finish_kernel(n, m, x_ref, part_ref, r_ref, total_ref, row, grid, sems):
    send_sem, recv_sem, seq_send, seq_recv, head_send, head_recv, own_sem = sems
    me, peers = others("seq", n)
    my_head, head_peers = others("head", m)
    own = pltpu.make_async_copy(x_ref.at[me], r_ref.at[me], own_sem.at[0])
    own.start()
    mine = pltpu.make_async_copy(part_ref, row.at[me], own_sem.at[1])
    mine.start()
    greet([{"seq": p} for p in peers] + [{"head": p} for p in head_peers])
    parts = [
        send(part_ref, row.at[me], seq_send.at[k], seq_recv.at[k], {"seq": p})
        for k, p in enumerate(peers)
    ]
    copies = [
        send(x_ref.at[p], r_ref.at[me], send_sem.at[k], recv_sem.at[k], {"seq": p})
        for k, p in enumerate(peers)
    ]
    mine.wait()
    for copy in parts:
        copy.wait()
    keep = pltpu.make_async_copy(row, grid.at[my_head], own_sem.at[1])
    keep.start()
    rows = [
        send(row, grid.at[my_head], head_send.at[k], head_recv.at[k], {"head": p})
        for k, p in enumerate(head_peers)
    ]
    keep.wait()
    for copy in rows:
        copy.wait()
    total_ref[...] = jnp.sum(jnp.sum(grid[...], axis=(0, 1)), axis=1, keepdims=True)
    own.wait()
    for copy in copies:
        copy.wait()


def finish(x, part, n, m):
    any_space = pl.BlockSpec(memory_space=pl.ANY)
    dma = pltpu.SemaphoreType.DMA
    return pl.pallas_call(
        functools.partial(finish_kernel, n, m),
        out_shape=(
            jax.ShapeDtypeStruct(x.shape, x.dtype),
            jax.ShapeDtypeStruct((1, 1), F32),
        ),
        in_specs=[any_space, any_space],
        out_specs=(any_space, pl.BlockSpec(memory_space=pltpu.VMEM)),
        scratch_shapes=[
            pltpu.VMEM((n, 1, LANES), F32),
            pltpu.VMEM((m, n, 1, LANES), F32),
            [
                dma((n - 1,)), dma((n - 1,)), dma((n - 1,)), dma((n - 1,)),
                dma((m - 1,)), dma((m - 1,)), dma((2,)),
            ],
        ],
        compiler_params=pltpu.CompilerParams(collective_id=1, has_side_effects=True),
    )(x, part)


def head_kernel(dt, ds, counts, x_ref, g_ref, part_ref, packed, rows, t_ref, s_ref, grad):
    blocks = x_ref.shape[0]
    depth = dt + ds
    scale = ds ** -0.5
    t_scale, s_scale = dt ** -0.5 * LOG2E, scale * LOG2E
    lane = lax.broadcasted_iota(jnp.int32, (depth, LANES), 1)

    packed[...] = jnp.zeros_like(packed)
    start = jnp.int32(0)
    for b in range(blocks):
        shift = lax.rem(start, LANES)
        base = pl.multiple_of(start - shift, LANES)
        first = pltpu.roll(x_ref[b, :, :LANES].astype(F32), shift, 1)
        second = pltpu.roll(x_ref[b, :, LANES:].astype(F32), shift, 1)
        late = lane >= shift
        here = pl.ds(base, LANES)
        packed[:depth, here] = jnp.where(late, first, packed[:depth, here])
        packed[:depth, pl.ds(base + LANES, LANES)] = jnp.where(late, second, first)
        packed[:depth, pl.ds(base + 2 * LANES, LANES)] = second
        start = start + counts[b]
    for c in range(LIVE // TILE):
        here = slice(c * TILE, (c + 1) * TILE)
        rows[here, :] = packed[:, here].T.astype(BF16)
    grad[...] = jnp.zeros_like(grad)

    feature = lax.broadcasted_iota(jnp.int32, (LANES, TILE), 0)
    causal = lax.broadcasted_iota(jnp.int32, (TILE, TILE), 0) <= lax.broadcasted_iota(
        jnp.int32, (TILE, TILE), 1
    )

    def at(c):
        return pl.ds(pl.multiple_of(c * TILE, TILE), TILE)

    def row_block(i, loss):
        query = packed[:, at(i)]
        t_query = jnp.where(feature < dt, query, 0.0).astype(BF16)
        s_query = jnp.where(feature < dt, 0.0, query).astype(BF16)
        s_own = query[dt:depth].astype(BF16)

        def logits(j):
            key = rows[at(j), :]
            t = jnp.dot(key, t_query, preferred_element_type=F32) * t_scale
            s = jnp.dot(key, s_query, preferred_element_type=F32) * s_scale
            return t, s

        t, s = logits(i)
        t = jnp.where(causal, t, NEGATIVE)
        s = jnp.where(causal, s, NEGATIVE)
        t_ref[at(i), :] = t
        s_ref[at(i), :] = s

        def fold(v, op):
            return op(v.reshape(TILE // 8, 8, TILE), axis=0)

        def tops(j, tops_so_far):
            t, s = logits(j)
            t_ref[at(j), :] = t
            s_ref[at(j), :] = s
            return (
                jnp.maximum(tops_so_far[0], fold(t, jnp.max)),
                jnp.maximum(tops_so_far[1], fold(s, jnp.max)),
            )

        t_top, s_top = lax.fori_loop(0, i, tops, (fold(t, jnp.max), fold(s, jnp.max)))
        t_top = jnp.max(t_top, axis=0, keepdims=True)
        s_top = jnp.max(s_top, axis=0, keepdims=True)

        def sums(j, so_far):
            t, s = t_ref[at(j), :], s_ref[at(j), :]
            pt = jnp.exp2(t - t_top)
            ps = jnp.exp2(s - s_top)
            t_ref[at(j), :] = pt
            s_ref[at(j), :] = ps
            return (
                so_far[0] + fold(pt, jnp.sum),
                so_far[1] + fold(ps, jnp.sum),
                so_far[2] + fold(pt * (t - s), jnp.sum),
            )

        zero = jnp.zeros((8, TILE), F32)
        t_sum, s_sum, cross = (
            jnp.sum(v, axis=0, keepdims=True)
            for v in lax.fori_loop(0, i + 1, sums, (zero, zero, zero))
        )
        kl = cross / t_sum - (t_top + jnp.log2(t_sum)) + (s_top + jnp.log2(s_sum))
        t_inv, s_inv = 1.0 / t_sum, 1.0 / s_sum

        def grads(j, query_grad):
            w = (s_ref[at(j), :] * s_inv - t_ref[at(j), :] * t_inv).astype(BF16)
            s_key = packed[dt:depth, at(j)].astype(BF16)
            grad[:, at(j)] += lax.dot_general(
                s_own, w, (((1,), (1,)), ((), ())), preferred_element_type=F32
            )
            return query_grad + jnp.dot(s_key, w, preferred_element_type=F32)

        query_grad = lax.fori_loop(0, i + 1, grads, jnp.zeros((ds, TILE), F32))
        grad[:, at(i)] += query_grad
        return loss + kl * LN2

    loss = lax.fori_loop(0, LIVE // TILE, row_block, jnp.zeros((1, TILE), F32))
    part_ref[0] = loss[:, :LANES] + loss[:, LANES:]

    lane = lax.broadcasted_iota(jnp.int32, (ds, LANES), 1)
    start = jnp.int32(0)
    for b in range(blocks):
        shift = lax.rem(start, LANES)
        base = pl.multiple_of(start - shift, LANES)
        back = lax.rem(LANES - shift, LANES)
        pieces = [
            pltpu.roll(grad[:, pl.ds(base + k * LANES, LANES)], back, 1) for k in range(3)
        ]
        for k in range(2):
            v = jnp.where(lane < LANES - shift, pieces[k], pieces[k + 1])
            v = jnp.where(lane + k * LANES < counts[b], v * scale, 0.0)
            g_ref[b, :, k * LANES:(k + 1) * LANES] = v.astype(BF16)
        start = start + counts[b]


def one_head(counts, x, dt, ds):
    blocks, depth, width = x.shape
    padded = LIVE + 3 * LANES
    vmem = pl.BlockSpec(memory_space=pltpu.VMEM)
    return pl.pallas_call(
        functools.partial(head_kernel, dt, ds),
        out_shape=(
            jax.ShapeDtypeStruct((blocks, ds, width), BF16),
            jax.ShapeDtypeStruct((1, 1, LANES), F32),
        ),
        in_specs=[pl.BlockSpec(memory_space=pltpu.SMEM), vmem],
        out_specs=(vmem, vmem),
        scratch_shapes=[
            pltpu.VMEM((LANES, padded), F32),
            pltpu.VMEM((LIVE, LANES), BF16),
            pltpu.VMEM((LIVE, TILE), F32),
            pltpu.VMEM((LIVE, TILE), F32),
            pltpu.VMEM((ds, padded), F32),
        ],
        compiler_params=pltpu.CompilerParams(vmem_limit_bytes=48 << 20),
    )(counts, x)


def local(teacher, student, counts):
    n, m = lax.axis_size("seq"), lax.axis_size("head")
    tokens = teacher.shape[0]
    dt, ds = teacher.shape[1] // n, student.shape[1] // n

    def by_head(x, d):
        return x.reshape(tokens, n, d).transpose(1, 2, 0)

    x = jnp.concatenate([by_head(teacher, dt), by_head(student, ds)], axis=1)
    x = exchange(x, n)
    grad, part = one_head(counts, x, dt, ds)
    grad, total = finish(grad, part[0], n, m)
    grad = grad.transpose(2, 0, 1).reshape(tokens, n * ds).astype(F32)
    loss = total[0, 0] / (H_REL * jnp.sum(counts).astype(F32))
    return grad, loss


def solution(mesh):
    return jax.shard_map(
        local,
        mesh=mesh,
        in_specs=(P("seq", "head"), P("seq", "head"), P()),
        out_specs=(P("seq", "head"), P()),
        check_vma=False,
    )
```

```python
import functools

import jax
import jax.numpy as jnp
from jax import lax
from jax.experimental import pallas as pl
from jax.experimental.pallas import tpu as pltpu
from jax.sharding import PartitionSpec as P

H_REL = 128
LIVE = 3072
TILE = 256
LANES = 128
LOG2E = 1.4426950408889634
LN2 = 0.6931471805599453
NEGATIVE = -1e30
MESH = pl.DeviceIdType.MESH
F32 = jnp.float32
BF16 = jnp.bfloat16


def greet(peers):
    barrier = pltpu.get_barrier_semaphore()
    for peer in peers:
        pl.semaphore_signal(barrier, inc=1, device_id=peer, device_id_type=MESH)
    pl.semaphore_wait(barrier, len(peers))


def others(axis, n):
    me = lax.axis_index(axis)
    return me, [lax.rem(me + k, n) for k in range(1, n)]


def send(src, dst, send_sem, recv_sem, device):
    copy = pltpu.make_async_remote_copy(
        src_ref=src, dst_ref=dst, send_sem=send_sem, recv_sem=recv_sem,
        device_id=device, device_id_type=MESH,
    )
    copy.start()
    return copy


def own_start(counts, n):
    me = lax.axis_index("seq")
    start = jnp.int32(0)
    for b in range(n - 1):
        start = start + jnp.where(b < me, counts[b], 0)
    return me, lax.rem(start, TILE)


def enter_kernel(n, counts, t_ref, s_ref, o_ref):
    _, shift = own_start(counts, n)
    dt = t_ref.shape[1] // n
    for ref, row in ((t_ref, 0), (s_ref, dt)):
        d = ref.shape[1] // n
        for c in range(ref.shape[1] // LANES):
            part = ref[:, c * LANES:(c + 1) * LANES].astype(F32).T
            part = pltpu.roll(part, shift, 1).astype(BF16)
            for k in range(LANES // d):
                o_ref[c * (LANES // d) + k, row:row + d, :] = part[k * d:(k + 1) * d]


def leave_kernel(n, scale, counts, g_ref, total_ref, o_ref, loss_ref):
    me, shift = own_start(counts, n)
    back = lax.rem(TILE - shift, TILE)
    ds = g_ref.shape[1]
    per = LANES // ds
    lane = lax.broadcasted_iota(jnp.int32, (LANES, TILE), 1)
    real = jnp.int32(0)
    whole = jnp.int32(0)
    for b in range(n):
        real = real + jnp.where(b == me, counts[b], 0)
        whole = whole + counts[b]
    for c in range(n // per):
        part = g_ref[c * per:(c + 1) * per].astype(F32).reshape(LANES, TILE)
        part = jnp.where(lane < real, pltpu.roll(part, back, 1) * scale, 0.0)
        o_ref[:, c * LANES:(c + 1) * LANES] = part.T
    loss_ref[...] = total_ref[...] / (H_REL * whole.astype(F32))


def pack(starts, spare, x_ref, packed, rows, dt):
    blocks, depth, width = x_ref.shape
    lane = lax.broadcasted_iota(jnp.int32, (depth, TILE), 1)
    for c in range(LIVE // TILE):
        v = None
        for b in range(c, min(blocks, c + spare + 1)):
            piece = x_ref[b].astype(F32)
            v = piece if v is None else jnp.where(lane >= starts[b] - c * TILE, piece, v)
        here = slice(c * TILE, (c + 1) * TILE)
        packed[:, here] = v
        t, s = v[:dt], v[dt:]
        rows[here, :] = jnp.concatenate([t, t, t, s, s], axis=0).T.astype(BF16)


def pieces(x, count):
    out = []
    for k in range(count):
        out.append(x.astype(BF16))
        x = x - out[-1].astype(F32)
    return out


def at(c):
    return pl.ds(pl.multiple_of(c * TILE, TILE), TILE)


def tile_of(i, j):
    return lax.div(i * (i + 1), 2) + j


def fold(v, op):
    return op(v.reshape(TILE // 8, 8, TILE), axis=0)


def statistics(i, dt, packed, rows, pt_ref, ps_ref, tops, stats):
    ds = packed.shape[0] - dt
    query = packed[:, at(i)]
    t_query = pieces(query[:dt] * (dt ** -0.5 * LOG2E), 3)
    s_query = pieces(query[dt:] * (ds ** -0.5 * LOG2E), 2)
    t_zero, s_zero = jnp.zeros((3 * dt, TILE), BF16), jnp.zeros((2 * ds, TILE), BF16)
    t_query = jnp.concatenate(t_query + [s_zero], axis=0)
    s_query = jnp.concatenate([t_zero] + s_query, axis=0)
    causal = lax.broadcasted_iota(jnp.int32, (TILE, TILE), 0) <= lax.broadcasted_iota(
        jnp.int32, (TILE, TILE), 1
    )

    def one_tile(j, state, diagonal):
        key = rows[at(j), :]
        t = jnp.dot(key, t_query, preferred_element_type=F32)
        s = jnp.dot(key, s_query, preferred_element_type=F32)
        if diagonal:
            t = jnp.where(causal, t, NEGATIVE)
            s = jnp.where(causal, s, NEGATIVE)
        t = t.reshape(TILE // 8, 8, TILE)
        s = s.reshape(TILE // 8, 8, TILE)
        t_top, s_top = jnp.max(t, axis=0), jnp.max(s, axis=0)
        if not diagonal:
            t_top = jnp.maximum(t_top, state[0])
            s_top = jnp.maximum(s_top, state[1])
        pt = jnp.exp2(t - t_top)
        ps = jnp.exp2(s - s_top)
        here = tile_of(i, j)
        pt_ref[here] = pt
        ps_ref[here] = ps
        tops[here, 0] = t_top
        tops[here, 1] = s_top
        t_sum, s_sum = jnp.sum(pt, axis=0), jnp.sum(ps, axis=0)
        cross = jnp.sum(pt * (t - s), axis=0)
        if not diagonal:
            t_less = jnp.exp2(state[0] - t_top)
            t_sum = t_sum + state[2] * t_less
            cross = cross + state[3] * t_less
            s_sum = s_sum + state[4] * jnp.exp2(state[1] - s_top)
        return t_top, s_top, t_sum, cross, s_sum

    state = one_tile(i, None, True)
    t8, s8, t_sum, cross, s_sum = lax.fori_loop(
        0, i, lambda j, state: one_tile(j, state, False), state
    )
    t_top = jnp.max(t8, axis=0, keepdims=True)
    s_top = jnp.max(s8, axis=0, keepdims=True)
    t_less = jnp.exp2(t8 - t_top)
    t_sum = jnp.sum(t_sum * t_less, axis=0, keepdims=True)
    cross = jnp.sum(cross * t_less, axis=0, keepdims=True)
    s_sum = jnp.sum(s_sum * jnp.exp2(s8 - s_top), axis=0, keepdims=True)
    kl = cross / t_sum - (t_top + jnp.log2(t_sum)) + (s_top + jnp.log2(s_sum))
    stats[i] = jnp.concatenate([t_top, s_top, 1.0 / t_sum, 1.0 / s_sum], axis=0)
    return kl * LN2


def gradients(i, dt, packed, pt_ref, ps_ref, tops, stats, grad):
    s_own = packed[dt:, at(i)].astype(BF16)
    t_top, s_top, t_inv, s_inv = (stats[i, pl.ds(k, 1), :] for k in range(4))

    def one_tile(j, query_grad):
        here = tile_of(i, j)
        t_scale = jnp.exp2(tops[here, 0] - t_top) * t_inv
        s_scale = jnp.exp2(tops[here, 1] - s_top) * s_inv
        w = ps_ref[here] * s_scale - pt_ref[here] * t_scale
        w = w.reshape(TILE, TILE).astype(BF16)
        s_key = packed[dt:, at(j)].astype(BF16)
        grad[j] += lax.dot_general(
            s_own, w, (((1,), (1,)), ((), ())), preferred_element_type=F32
        )
        return query_grad + jnp.dot(s_key, w, preferred_element_type=F32)

    query_grad = lax.fori_loop(0, i + 1, one_tile, jnp.zeros(grad.shape[1:], F32))
    grad[i] += query_grad


def kernel(
    dt, n, m, counts, x_ref, g_ref, total_ref,
    x_in, packed, rows, pt_ref, ps_ref, tops, stats, grad, g_out, starts, part, row, grid, sems,
):
    x_send, x_recv, g_send, g_recv, seq_send, seq_recv, head_send, head_recv, own = sems
    blocks = LIVE // TILE
    spare = n - blocks
    me, peers = others("seq", n)
    my_head, head_peers = others("head", m)
    own_x = pltpu.make_async_copy(x_ref.at[me], x_in.at[me], own.at[0])
    own_x.start()
    greet([{"seq": p} for p in peers] + [{"head": p} for p in head_peers])
    copies = [
        send(x_ref.at[p], x_in.at[me], x_send.at[k], x_recv.at[k], {"seq": p})
        for k, p in enumerate(peers)
    ]
    start = jnp.int32(0)
    scalars = []
    for b in range(n):
        starts[b] = start
        scalars.append(start)
        start = start + counts[b]
    grad[...] = jnp.zeros_like(grad)
    own_x.wait()
    for copy in copies:
        copy.wait()

    pack(scalars, spare, x_in, packed, rows, dt)
    loss = lax.fori_loop(
        0, blocks,
        lambda i, loss: loss + statistics(i, dt, packed, rows, pt_ref, ps_ref, tops, stats),
        jnp.zeros((1, TILE), F32),
    )
    part[...] = loss[:, :LANES] + loss[:, LANES:]

    def finish_block(b):
        lane = lax.broadcasted_iota(jnp.int32, grad.shape[1:], 1)
        first = starts[b]
        top = blocks - 1
        v = grad[jnp.minimum(b, top)]
        for k in range(1, spare + 1):
            c = jnp.clip(b - k, 0, top)
            v = jnp.where(lane + c * TILE >= first, grad[c], v)
        g_out[b] = v.astype(BF16)

    def to_owner(b):
        @pl.when(b == me)
        def _():
            pltpu.make_async_copy(g_out.at[b], g_ref.at[me], own.at[1]).start()

        @pl.when(b != me)
        def _():
            send(g_out.at[b], g_ref.at[me], g_send.at[b], g_recv.at[me], {"seq": b})

    def down(k, _):
        i = blocks - 1 - k
        gradients(i, dt, packed, pt_ref, ps_ref, tops, stats, grad)

        @pl.when(k > 0)
        def _():
            to_owner(i + spare + 1)

        finish_block(i + spare)
        return 0

    lax.fori_loop(0, 1, down, 0)
    own_part = pltpu.make_async_copy(part, row.at[me], own.at[0])
    own_part.start()
    parts = [
        send(part, row.at[me], seq_send.at[k], seq_recv.at[k], {"seq": p})
        for k, p in enumerate(peers)
    ]
    lax.fori_loop(1, 6, down, 0)
    own_part.wait()
    for copy in parts:
        copy.wait()
    own_row = pltpu.make_async_copy(row, grid.at[my_head], own.at[0])
    own_row.start()
    row_copies = [
        send(row, grid.at[my_head], head_send.at[k], head_recv.at[k], {"head": p})
        for k, p in enumerate(head_peers)
    ]
    lax.fori_loop(6, blocks, down, 0)
    for b in range(spare):
        finish_block(b)
    for b in range(spare, -1, -1):
        to_owner(b)
    own_row.wait()
    for copy in row_copies:
        copy.wait()
    total_ref[...] = jnp.sum(jnp.sum(grid[...], axis=(0, 1)), axis=1, keepdims=True)
    pltpu.make_async_copy(g_out.at[me], g_ref.at[me], own.at[1]).wait()
    for p in peers:
        pltpu.make_async_remote_copy(
            src_ref=g_out.at[p], dst_ref=g_ref.at[p], send_sem=g_send.at[p],
            recv_sem=g_recv.at[p], device_id={"seq": p}, device_id_type=MESH,
        ).wait()


def local(teacher, student, counts):
    n, m = lax.axis_size("seq"), lax.axis_size("head")
    tokens = teacher.shape[0]
    dt, ds = teacher.shape[1] // n, student.shape[1] // n
    depth = dt + ds
    blocks = LIVE // TILE
    tiles = blocks * (blocks + 1) // 2
    vmem = pl.BlockSpec(memory_space=pltpu.VMEM)
    smem = pl.BlockSpec(memory_space=pltpu.SMEM)
    any_space = pl.BlockSpec(memory_space=pl.ANY)
    dma = pltpu.SemaphoreType.DMA
    x = pl.pallas_call(
        functools.partial(enter_kernel, n),
        out_shape=jax.ShapeDtypeStruct((n, depth, tokens), BF16),
        in_specs=[smem, vmem, vmem],
        out_specs=vmem,
    )(counts, teacher, student)
    grad, total = pl.pallas_call(
        functools.partial(kernel, dt, n, m),
        out_shape=(
            jax.ShapeDtypeStruct((n, ds, tokens), BF16),
            jax.ShapeDtypeStruct((1, 1), F32),
        ),
        in_specs=[smem, any_space],
        out_specs=(any_space, vmem),
        scratch_shapes=[
            pltpu.VMEM((n, depth, tokens), BF16),
            pltpu.VMEM((depth, LIVE), F32),
            pltpu.VMEM((LIVE, 3 * dt + 2 * ds), BF16),
            pltpu.VMEM((tiles, TILE // 8, 8, TILE), F32),
            pltpu.VMEM((tiles, TILE // 8, 8, TILE), F32),
            pltpu.VMEM((tiles, 2, 8, TILE), F32),
            pltpu.VMEM((blocks, 4, TILE), F32),
            pltpu.VMEM((blocks, ds, TILE), F32),
            pltpu.VMEM((n, ds, tokens), BF16),
            pltpu.SMEM((n,), jnp.int32),
            pltpu.VMEM((1, LANES), F32),
            pltpu.VMEM((n, 1, LANES), F32),
            pltpu.VMEM((m, n, 1, LANES), F32),
            [dma((n - 1,))] * 2 + [dma((n,))] * 2 + [dma((n - 1,))] * 2
            + [dma((m - 1,))] * 2 + [dma((2,))],
        ],
        compiler_params=pltpu.CompilerParams(
            collective_id=0, has_side_effects=True, vmem_limit_bytes=60 << 20
        ),
    )(counts, x)
    grad, loss = pl.pallas_call(
        functools.partial(leave_kernel, n, ds ** -0.5),
        out_shape=(
            jax.ShapeDtypeStruct((tokens, n * ds), F32),
            jax.ShapeDtypeStruct((1, 1), F32),
        ),
        in_specs=[smem, vmem, vmem],
        out_specs=(vmem, vmem),
    )(counts, grad, total)
    return grad, loss.reshape(())


def solution(mesh):
    return jax.shard_map(
        local,
        mesh=mesh,
        in_specs=(P("seq", "head"), P("seq", "head"), P()),
        out_specs=(P("seq", "head"), P()),
        check_vma=False,
    )
```

```python
import functools

import jax
import jax.numpy as jnp
from jax import lax
from jax.experimental import pallas as pl
from jax.experimental.pallas import tpu as pltpu
from jax.sharding import PartitionSpec as P

H_REL = 128
LIVE = 3072
TILE = 256
LANES = 128
LOG2E = 1.4426950408889634
LN2 = 0.6931471805599453
NEGATIVE = -1e30
MESH = pl.DeviceIdType.MESH
F32 = jnp.float32
BF16 = jnp.bfloat16


def greet(peers):
    barrier = pltpu.get_barrier_semaphore()
    for peer in peers:
        pl.semaphore_signal(barrier, inc=1, device_id=peer, device_id_type=MESH)
    pl.semaphore_wait(barrier, len(peers))


def others(axis, n):
    me = lax.axis_index(axis)
    return me, [lax.rem(me + k, n) for k in range(1, n)]


def send(src, dst, send_sem, recv_sem, device):
    copy = pltpu.make_async_remote_copy(
        src_ref=src, dst_ref=dst, send_sem=send_sem, recv_sem=recv_sem,
        device_id=device, device_id_type=MESH,
    )
    copy.start()
    return copy


def own_start(counts, n):
    me = lax.axis_index("seq")
    start = jnp.int32(0)
    for b in range(n - 1):
        start = start + jnp.where(b < me, counts[b], 0)
    return me, lax.rem(start, TILE)


def enter_kernel(n, counts, t_ref, s_ref, o_ref):
    _, shift = own_start(counts, n)
    dt = t_ref.shape[1] // n
    for ref, row in ((t_ref, 0), (s_ref, dt)):
        d = ref.shape[1] // n
        for c in range(ref.shape[1] // LANES):
            part = ref[:, c * LANES:(c + 1) * LANES].astype(F32).T
            part = pltpu.roll(part, shift, 1).astype(BF16)
            for k in range(LANES // d):
                o_ref[c * (LANES // d) + k, row:row + d, :] = part[k * d:(k + 1) * d]


def leave_kernel(n, scale, counts, g_ref, total_ref, o_ref, loss_ref):
    me, shift = own_start(counts, n)
    back = lax.rem(TILE - shift, TILE)
    ds = g_ref.shape[1]
    per = LANES // ds
    lane = lax.broadcasted_iota(jnp.int32, (LANES, TILE), 1)
    real = jnp.int32(0)
    whole = jnp.int32(0)
    for b in range(n):
        real = real + jnp.where(b == me, counts[b], 0)
        whole = whole + counts[b]
    for c in range(n // per):
        part = g_ref[c * per:(c + 1) * per].astype(F32).reshape(LANES, TILE)
        part = jnp.where(lane < real, pltpu.roll(part, back, 1) * scale, 0.0)
        o_ref[:, c * LANES:(c + 1) * LANES] = part.T
    loss_ref[...] = total_ref[...] / (H_REL * whole.astype(F32))


def pack(starts, spare, x_ref, students, rows, weights, dt):
    blocks, depth, width = x_ref.shape
    ds = depth - dt
    lane = lax.broadcasted_iota(jnp.int32, (depth, TILE), 1)
    for c in range(LIVE // TILE):
        v = None
        for b in range(c, min(blocks, c + spare + 1)):
            piece = x_ref[b].astype(F32)
            v = piece if v is None else jnp.where(lane >= starts[b] - c * TILE, piece, v)
        t, s = v[:dt], v[dt:]
        rows[c] = jnp.concatenate([t, t, s, s, s, s], axis=0).T.astype(BF16)
        students[c] = s.astype(BF16)
        weights[c, 0] = jnp.concatenate(pieces(t * (dt ** -0.5 * LOG2E), 2), axis=0)
        weights[c, 1] = jnp.concatenate(
            pieces(s * (ds ** -0.5 * LOG2E), 3) + [jnp.zeros((ds, TILE), BF16)], axis=0
        )


def pieces(x, count):
    out = []
    for k in range(count):
        out.append(x.astype(BF16))
        x = x - out[-1].astype(F32)
    return out


def at(c):
    return pl.ds(pl.multiple_of(c * TILE, TILE), TILE)


def tile_of(i, j):
    return lax.div(i * (i + 1), 2) + j


def step(later, now, diagonal, rows, weights, into, source, tops, running, state, pt_ref, ps_ref):
    now_at = [tile_of(*c) for c in now]
    now_top = [(tops[here, 0], tops[here, 1]) for here in now_at]
    sums = [[jnp.zeros(tops.shape[2:], F32)] * 3 for _ in now]
    made = []
    for i, j in later:
        key = rows[j]
        made.append([
            jnp.dot(
                key[:, k * LANES:(k + 1) * LANES], weights[i, k], preferred_element_type=F32
            )
            for k in range(2)
        ])
    tallest = [[None, None] for _ in later]
    for g in range(TILE // 8):
        for u, here in enumerate(now_at):
            t, s = source[u, 0, g], source[u, 1, g]
            pt = jnp.exp2(t - now_top[u][0])
            ps = jnp.exp2(s - now_top[u][1])
            pt_ref[here, g] = pt
            ps_ref[here, g] = ps
            sums[u] = [sums[u][0] + pt, sums[u][1] + ps, sums[u][2] + pt * (t - s)]
        for u in range(len(later)):
            for k in range(2):
                v = made[u][k][g * 8:(g + 1) * 8]
                if diagonal:
                    row = lax.broadcasted_iota(jnp.int32, v.shape, 0) + g * 8
                    v = jnp.where(row <= lax.broadcasted_iota(jnp.int32, v.shape, 1), v, NEGATIVE)
                into[u, k, g] = v
                tallest[u][k] = v if g == 0 else jnp.maximum(tallest[u][k], v)
    for u, (i, j) in enumerate(later):
        for k in range(2):
            top = jnp.maximum(tallest[u][k], running[i, k])
            running[i, k] = top
            tops[tile_of(i, j), k] = top
    for u, (i, _) in enumerate(now):
        t_top, s_top = now_top[u]
        t_less = jnp.exp2(state[i, 0] - t_top)
        s_less = jnp.exp2(state[i, 1] - s_top)
        state[i, 0] = t_top
        state[i, 1] = s_top
        state[i, 2] = state[i, 2] * t_less + sums[u][0]
        state[i, 3] = state[i, 3] * s_less + sums[u][1]
        state[i, 4] = state[i, 4] * t_less + sums[u][2]


def by_parity(count, even, odd, run):
    @pl.when(lax.rem(count, 2) == 0)
    def _():
        run(even, odd)

    @pl.when(lax.rem(count, 2) == 1)
    def _():
        run(odd, even)


def statistics(rows, weights, even, odd, pt_ref, ps_ref, tops, running, state, stats):
    blocks = rows.shape[0]
    running[...] = jnp.full(running.shape, NEGATIVE, F32)
    state[:, :2] = jnp.full(running.shape, NEGATIVE, F32)
    state[:, 2:] = jnp.zeros((blocks, 3, *running.shape[2:]), F32)

    def sweep(first, after, tiles, diagonal):
        def one(later, now, into, source):
            step(
                later, now, diagonal, rows, weights, into, source, tops, running, state,
                pt_ref, ps_ref,
            )

        def trip(count, now):
            later = [after(*now[-1])]
            later.append(after(*later[0]))
            by_parity(count, even, odd, lambda source, into: one(later, now, into, source))
            return later

        first = (jnp.int32(first[0]), jnp.int32(first[1]))
        first = [first, after(*first)]
        one(first, [], even, None)
        trips = tiles // 2 - 1
        now = lax.fori_loop(0, trips, trip, first)
        one([], now, None, odd if trips % 2 else even)

    def below(i, j):
        wrap = j + 1 == i
        return jnp.where(wrap, i + 1, i), jnp.where(wrap, 0, j + 1)

    sweep((0, 0), lambda i, j: (i + 1, j + 1), blocks, True)
    sweep((1, 0), below, blocks * (blocks - 1) // 2, False)

    t8, s8, t_sum, s_sum, cross = (state[:, k] for k in range(5))
    t_top = jnp.max(t8, axis=1, keepdims=True)
    s_top = jnp.max(s8, axis=1, keepdims=True)
    t_less = jnp.exp2(t8 - t_top)
    t_sum = jnp.sum(t_sum * t_less, axis=1, keepdims=True)
    cross = jnp.sum(cross * t_less, axis=1, keepdims=True)
    s_sum = jnp.sum(s_sum * jnp.exp2(s8 - s_top), axis=1, keepdims=True)
    kl = cross / t_sum - (t_top + jnp.log2(t_sum)) + (s_top + jnp.log2(s_sum))
    stats[...] = jnp.concatenate([t_top, s_top, 1.0 / t_sum, 1.0 / s_sum], axis=1)
    return jnp.sum(kl, axis=0) * LN2


def back(i, j):
    wrap = j == i
    return jnp.where(wrap, i - 1, i), jnp.where(wrap, 0, j + 1)


def gradient_step(later, now, into, source, students, pt_ref, ps_ref, tops, stats, grad):
    nt = (((1,), (1,)), ((), ()))
    parts = [
        (
            lax.dot_general(students[i], source[u], nt, preferred_element_type=F32),
            jnp.dot(students[j], source[u], preferred_element_type=F32),
        )
        for u, (i, j) in enumerate(now)
    ]
    for u, (i, j) in enumerate(later):
        here = tile_of(i, j)
        t_top, s_top, t_inv, s_inv = (stats[i, pl.ds(k, 1), :] for k in range(4))
        t_scale = jnp.exp2(tops[here, 0] - t_top) * t_inv
        s_scale = jnp.exp2(tops[here, 1] - s_top) * s_inv
        for g in range(0, TILE // 8, 2):
            w = ps_ref[here, g:g + 2] * s_scale - pt_ref[here, g:g + 2] * t_scale
            into[u, g * 8:g * 8 + 16, :] = w.reshape(16, TILE).astype(BF16)
    for (i, j), (key_grad, query_grad) in zip(now, parts):
        grad[j] += key_grad
        grad[i] += query_grad


def gradients(first, last, final, now, even, odd, students, pt_ref, ps_ref, tops, stats, grad, row_done):
    def one(later, now, into, source):
        gradient_step(later, now, into, source, students, pt_ref, ps_ref, tops, stats, grad)

    def check(now):
        for i, j in now:
            pl.when(i == j)(functools.partial(row_done, i))

    def trip(count, now):
        later = [back(*now[-1])]
        later.append(back(*later[0]))
        by_parity(count, even, odd, lambda source, into: one(later, now, into, source))
        check(now)
        return later

    now = lax.fori_loop(first, last - final, trip, now)
    if final:
        one([], now, None, odd if (last - 1) % 2 else even)
        check(now)
    return now


def compute_scratch(dt, ds):
    blocks = LIVE // TILE
    tiles = blocks * (blocks + 1) // 2
    return [
        pltpu.VMEM((blocks, ds, TILE), BF16),
        pltpu.VMEM((blocks, TILE, 2 * LANES), BF16),
        pltpu.VMEM((blocks, 2, LANES, TILE), BF16),
        pltpu.VMEM((2, 2, TILE // 8, 8, TILE), F32),
        pltpu.VMEM((2, 2, TILE // 8, 8, TILE), F32),
        pltpu.VMEM((tiles, TILE // 8, 8, TILE), F32),
        pltpu.VMEM((tiles, TILE // 8, 8, TILE), F32),
        pltpu.VMEM((tiles, 2, 8, TILE), F32),
        pltpu.VMEM((blocks, 2, 8, TILE), F32),
        pltpu.VMEM((blocks, 5, 8, TILE), F32),
        pltpu.VMEM((blocks, 4, TILE), F32),
        pltpu.VMEM((2, TILE, TILE), BF16),
        pltpu.VMEM((2, TILE, TILE), BF16),
        pltpu.VMEM((blocks, ds, TILE), F32),
    ]


def kernel(
    dt, n, m, counts, x_ref, g_ref, total_ref,
    x_in, students, rows, weights, even, odd, pt_ref, ps_ref, tops, running, state, stats,
    w_even, w_odd, grad, g_out, starts, part, row, grid, sems,
):
    x_send, x_recv, g_send, g_recv, seq_send, seq_recv, head_send, head_recv, own = sems
    blocks = LIVE // TILE
    spare = n - blocks
    me, peers = others("seq", n)
    my_head, head_peers = others("head", m)
    own_x = pltpu.make_async_copy(x_ref.at[me], x_in.at[me], own.at[0])
    own_x.start()
    greet([{"seq": p} for p in peers] + [{"head": p} for p in head_peers])
    copies = [
        send(x_ref.at[p], x_in.at[me], x_send.at[k], x_recv.at[k], {"seq": p})
        for k, p in enumerate(peers)
    ]
    start = jnp.int32(0)
    scalars = []
    for b in range(n):
        starts[b] = start
        scalars.append(start)
        start = start + counts[b]
    grad[...] = jnp.zeros_like(grad)
    own_x.wait()
    for copy in copies:
        copy.wait()

    pack(scalars, spare, x_in, students, rows, weights, dt)
    loss = statistics(rows, weights, even, odd, pt_ref, ps_ref, tops, running, state, stats)
    part[...] = loss[:, :LANES] + loss[:, LANES:]

    def finish_block(b):
        lane = lax.broadcasted_iota(jnp.int32, grad.shape[1:], 1)
        first = starts[b]
        top = blocks - 1
        v = grad[jnp.minimum(b, top)]
        for k in range(1, spare + 1):
            c = jnp.clip(b - k, 0, top)
            v = jnp.where(lane + c * TILE >= first, grad[c], v)
        g_out[b] = v.astype(BF16)

    def to_owner(b):
        @pl.when(b == me)
        def _():
            pltpu.make_async_copy(g_out.at[b], g_ref.at[me], own.at[1]).start()

        @pl.when(b != me)
        def _():
            send(g_out.at[b], g_ref.at[me], g_send.at[b], g_recv.at[me], {"seq": b})

    def row_done(i):
        @pl.when(i + spare + 1 < n)
        def _():
            to_owner(i + spare + 1)

        finish_block(i + spare)

    def run(first, last, final, now):
        return gradients(
            first, last, final, now, w_even, w_odd, students, pt_ref, ps_ref, tops, stats, grad, row_done
        )

    pairs = blocks * (blocks + 1) // 4
    now = (jnp.int32(blocks - 1), jnp.int32(0))
    now = [now, back(*now)]
    gradient_step(now, [], w_even, None, students, pt_ref, ps_ref, tops, stats, grad)
    own_part = pltpu.make_async_copy(part, row.at[me], own.at[0])
    own_part.start()
    parts = [
        send(part, row.at[me], seq_send.at[k], seq_recv.at[k], {"seq": p})
        for k, p in enumerate(peers)
    ]
    now = run(0, pairs // 2, False, now)
    own_part.wait()
    for copy in parts:
        copy.wait()
    own_row = pltpu.make_async_copy(row, grid.at[my_head], own.at[0])
    own_row.start()
    row_copies = [
        send(row, grid.at[my_head], head_send.at[k], head_recv.at[k], {"head": p})
        for k, p in enumerate(head_peers)
    ]
    run(pairs // 2, pairs, True, now)
    for b in range(spare):
        finish_block(b)
    for b in range(spare, -1, -1):
        to_owner(b)
    own_row.wait()
    for copy in row_copies:
        copy.wait()
    total_ref[...] = jnp.sum(jnp.sum(grid[...], axis=(0, 1)), axis=1, keepdims=True)
    pltpu.make_async_copy(g_out.at[me], g_ref.at[me], own.at[1]).wait()
    for p in peers:
        pltpu.make_async_remote_copy(
            src_ref=g_out.at[p], dst_ref=g_ref.at[p], send_sem=g_send.at[p],
            recv_sem=g_recv.at[p], device_id={"seq": p}, device_id_type=MESH,
        ).wait()


def local(teacher, student, counts):
    n, m = lax.axis_size("seq"), lax.axis_size("head")
    tokens = teacher.shape[0]
    dt, ds = teacher.shape[1] // n, student.shape[1] // n
    depth = dt + ds
    vmem = pl.BlockSpec(memory_space=pltpu.VMEM)
    smem = pl.BlockSpec(memory_space=pltpu.SMEM)
    any_space = pl.BlockSpec(memory_space=pl.ANY)
    dma = pltpu.SemaphoreType.DMA
    x = pl.pallas_call(
        functools.partial(enter_kernel, n),
        out_shape=jax.ShapeDtypeStruct((n, depth, tokens), BF16),
        in_specs=[smem, vmem, vmem],
        out_specs=vmem,
    )(counts, teacher, student)
    grad, total = pl.pallas_call(
        functools.partial(kernel, dt, n, m),
        out_shape=(
            jax.ShapeDtypeStruct((n, ds, tokens), BF16),
            jax.ShapeDtypeStruct((1, 1), F32),
        ),
        in_specs=[smem, any_space],
        out_specs=(any_space, vmem),
        scratch_shapes=[
            pltpu.VMEM((n, depth, tokens), BF16),
            *compute_scratch(dt, ds),
            pltpu.VMEM((n, ds, tokens), BF16),
            pltpu.SMEM((n,), jnp.int32),
            pltpu.VMEM((1, LANES), F32),
            pltpu.VMEM((n, 1, LANES), F32),
            pltpu.VMEM((m, n, 1, LANES), F32),
            [dma((n - 1,))] * 2 + [dma((n,))] * 2 + [dma((n - 1,))] * 2
            + [dma((m - 1,))] * 2 + [dma((2,))],
        ],
        compiler_params=pltpu.CompilerParams(
            collective_id=0, has_side_effects=True, vmem_limit_bytes=60 << 20
        ),
    )(counts, x)
    grad, loss = pl.pallas_call(
        functools.partial(leave_kernel, n, ds ** -0.5),
        out_shape=(
            jax.ShapeDtypeStruct((tokens, n * ds), F32),
            jax.ShapeDtypeStruct((1, 1), F32),
        ),
        in_specs=[smem, vmem, vmem],
        out_specs=(vmem, vmem),
    )(counts, grad, total)
    return grad, loss.reshape(())


def solution(mesh):
    return jax.shard_map(
        local,
        mesh=mesh,
        in_specs=(P("seq", "head"), P("seq", "head"), P()),
        out_specs=(P("seq", "head"), P()),
        check_vma=False,
    )
```

```python
import functools

import jax
import jax.numpy as jnp
from jax import lax
from jax.experimental import pallas as pl
from jax.experimental.pallas import tpu as pltpu
from jax.sharding import PartitionSpec as P

H_REL = 128
LIVE = 3072
STUDENT_TILES = 6
TEACHER_TILES = 6
GRADIENT_TILES = 6
TILE = 256
LANES = 128
LOG2E = 1.4426950408889634
LN2 = 0.6931471805599453
NEGATIVE = -1e30
MESH = pl.DeviceIdType.MESH
F32 = jnp.float32
BF16 = jnp.bfloat16


def others(axis, n):
    me = lax.axis_index(axis)
    return me, [lax.rem(me + k, n) for k in range(1, n)]


def send(src, dst, send_sem, recv_sem, device):
    copy = pltpu.make_async_remote_copy(
        src_ref=src, dst_ref=dst, send_sem=send_sem, recv_sem=recv_sem,
        device_id=device, device_id_type=MESH,
    )
    copy.start()
    return copy


def pieces(x, count):
    out = []
    for k in range(count):
        out.append(x.astype(BF16))
        x = x - out[-1].astype(F32)
    return out


def tile_of(i, j):
    return lax.shift_right_logical(i * (i + 1), 1) + j


def own_start(counts, n):
    me = lax.axis_index("seq")
    start, real = jnp.int32(0), jnp.int32(0)
    for b in range(n):
        start = start + jnp.where(b < me, counts[b], 0)
        real = real + jnp.where(b == me, counts[b], 0)
    return start & (TILE - 1), real


def turn(shift, count):
    row = lax.broadcasted_iota(jnp.int32, (TILE, TILE), 0)
    lane = lax.broadcasted_iota(jnp.int32, (TILE, TILE), 1)
    hit = (lane == ((row + shift) & (TILE - 1))) & (row < count)
    return jnp.where(hit, 1.0, 0.0).astype(BF16)


def enter(x_ref, turned, x_out):
    d = x_out.shape[1]
    for c in range(x_ref.shape[1] // LANES):
        part = lax.dot_general(
            x_ref[:, c * LANES:(c + 1) * LANES], turned, (((0,), (0,)), ((), ())),
            preferred_element_type=F32,
        ).astype(BF16)
        for k in range(LANES // d):
            x_out[c * (LANES // d) + k] = part[k * d:(k + 1) * d]


def pack(starts, spare, x_ref, plain, rows, weights, parts):
    blocks, d, _ = x_ref.shape
    lane = lax.broadcasted_iota(jnp.int32, (d, TILE), 1)
    fill = jnp.zeros((LANES - parts * d, TILE), BF16)
    for c in range(LIVE // TILE):
        v = None
        for b in range(c, min(blocks, c + spare + 1)):
            piece = x_ref[b].astype(F32)
            v = piece if v is None else jnp.where(lane >= starts[b] - c * TILE, piece, v)
        if plain is not None:
            plain[c] = v.astype(BF16)
        rows[c] = jnp.concatenate([v] * (LANES // d), axis=0).T.astype(BF16)
        split = pieces(v * (d ** -0.5 * LOG2E), parts)
        weights[c] = jnp.concatenate(split + [fill] if parts * d < LANES else split, axis=0)


def step(later, now, diagonal, rows, weights, into, source, tops, running, state, keep, other):
    now_at = [tile_of(*c) for c in now]
    now_top = [tops[here] for here in now_at]
    sums = [[jnp.zeros(tops.shape[1:], F32)] * 2 for _ in now]
    made = [jnp.dot(rows[j], weights[i], preferred_element_type=F32) for i, j in later]
    tallest = [None for _ in later]
    for u in range(max(len(now), len(later))):
        for g in range(TILE // 8):
            if now:
                v = source[u, g]
                p = jnp.exp2(v - now_top[u])
                sums[u] = [sums[u][0] + p, sums[u][1]]
                if other is None:
                    keep[now_at[u], g] = v
                else:
                    keep[now_at[u], g] = p
                    sums[u][1] = sums[u][1] + p * (v - other[now_at[u], g])
            if later:
                v = made[u][g * 8:(g + 1) * 8]
                if diagonal:
                    row = lax.broadcasted_iota(jnp.int32, v.shape, 0) + g * 8
                    v = jnp.where(row <= lax.broadcasted_iota(jnp.int32, v.shape, 1), v, NEGATIVE)
                into[u, g] = v
                tallest[u] = v if g == 0 else jnp.maximum(tallest[u], v)
    for u, (i, j) in enumerate(later):
        top = jnp.maximum(tallest[u], running[i])
        running[i] = top
        tops[tile_of(i, j)] = top
    for u, (i, _) in enumerate(now):
        less = jnp.exp2(state[i, 0] - now_top[u])
        state[i, 0] = now_top[u]
        state[i, 1] = state[i, 1] * less + sums[u][0]
        if other is not None:
            state[i, 2] = state[i, 2] * less + sums[u][1]


def by_parity(count, even, odd, run):
    @pl.when((count & 1) == 0)
    def _():
        run(even, odd)

    @pl.when((count & 1) == 1)
    def _():
        run(odd, even)


def chain(first, after, count):
    out = [first]
    while len(out) < count:
        out.append(after(*out[-1]))
    return out


def sweep(unit, rows, weights, even, odd, tops, running, state, keep, other):
    blocks = rows.shape[0]
    running[...] = jnp.full(running.shape, NEGATIVE, F32)
    state[:, :1] = jnp.full((blocks, 1, *running.shape[1:]), NEGATIVE, F32)
    state[:, 1:] = jnp.zeros((blocks, state.shape[1] - 1, *running.shape[1:]), F32)

    def run(first, after, tiles, diagonal):
        def one(later, now, into, source):
            step(
                later, now, diagonal, rows, weights, into, source, tops, running, state, keep,
                other,
            )

        def trip(count, now):
            later = chain(after(*now[-1]), after, unit)
            by_parity(count, even, odd, lambda source, into: one(later, now, into, source))
            return later

        now = chain((jnp.int32(first[0]), jnp.int32(first[1])), after, unit)
        one(now, [], even, None)
        trips = tiles // unit - 1
        now = lax.fori_loop(0, trips, trip, now)
        one([], now, None, odd if trips % 2 else even)

    def below(i, j):
        wrap = j + 1 == i
        return jnp.where(wrap, i + 1, i), jnp.where(wrap, 0, j + 1)

    run((0, 0), lambda i, j: (i + 1, j + 1), blocks, True)
    run((1, 0), below, blocks * (blocks - 1) // 2, False)


def totals(s_state, t_state, stats):
    def collect(state):
        top8 = state[:, 0]
        top = jnp.max(top8, axis=1, keepdims=True)
        less = jnp.exp2(top8 - top)
        return top, [
            jnp.sum(state[:, k] * less, axis=1, keepdims=True) for k in range(1, state.shape[1])
        ]

    s_top, (s_sum,) = collect(s_state)
    t_top, (t_sum, cross) = collect(t_state)
    s_lse = s_top + jnp.log2(s_sum)
    kl = cross / t_sum - (t_top + jnp.log2(t_sum)) + s_lse
    stats[...] = jnp.concatenate([s_lse, t_top, 1.0 / t_sum, s_lse], axis=1)
    return jnp.sum(kl, axis=0) * LN2


def back(i, j):
    wrap = j == i
    return jnp.where(wrap, i - 1, i), jnp.where(wrap, 0, j + 1)


def gradient_step(later, now, into, source, students, s_ref, pt_ref, tops, stats, grad):
    nt = (((1,), (1,)), ((), ()))
    parts = [
        (
            lax.dot_general(students[i], source[u], nt, preferred_element_type=F32),
            jnp.dot(students[j], source[u], preferred_element_type=F32),
        )
        for u, (i, j) in enumerate(now)
    ]
    for u, (i, j) in enumerate(later):
        here = tile_of(i, j)
        s_lse, t_top, t_inv = (stats[i, pl.ds(k, 1), :] for k in range(3))
        t_scale = jnp.exp2(tops[here] - t_top) * t_inv
        for g in range(0, TILE // 8, 2):
            w = jnp.exp2(s_ref[here, g:g + 2] - s_lse) - pt_ref[here, g:g + 2] * t_scale
            into[u, g * 8:g * 8 + 16, :] = w.reshape(16, TILE).astype(BF16)
    for (i, j), (key_grad, query_grad) in zip(now, parts):
        grad[j] += key_grad
        grad[i] += query_grad


def gradients(first, last, final, now, even, odd, row_done, *refs):
    def one(later, now, into, source):
        gradient_step(later, now, into, source, *refs)

    def check(now):
        for i, j in now:
            pl.when(i == j)(functools.partial(row_done, i))

    def trip(count, now):
        later = chain(back(*now[-1]), back, len(now))
        by_parity(count, even, odd, lambda source, into: one(later, now, into, source))
        check(now)
        return later

    now = lax.fori_loop(first, last - final, trip, now)
    if final:
        one([], now, None, odd if (last - 1) % 2 else even)
        check(now)
    return now


def compute_scratch(dt, ds):
    blocks = LIVE // TILE
    tiles = blocks * (blocks + 1) // 2
    groups = TILE // 8
    wide = max(STUDENT_TILES, TEACHER_TILES)
    return dict(
        students=pltpu.VMEM((blocks, ds, TILE), BF16),
        rows=pltpu.VMEM((2, blocks, TILE, LANES), BF16),
        weights=pltpu.VMEM((2, blocks, LANES, TILE), BF16),
        even=pltpu.VMEM((wide, groups, 8, TILE), F32),
        odd=pltpu.VMEM((wide, groups, 8, TILE), F32),
        s_ref=pltpu.VMEM((tiles, groups, 8, TILE), F32),
        pt_ref=pltpu.VMEM((tiles, groups, 8, TILE), F32),
        tops=pltpu.VMEM((tiles, 8, TILE), F32),
        running=pltpu.VMEM((blocks, 8, TILE), F32),
        s_state=pltpu.VMEM((blocks, 2, 8, TILE), F32),
        t_state=pltpu.VMEM((blocks, 3, 8, TILE), F32),
        stats=pltpu.VMEM((blocks, 4, TILE), F32),
        w_even=pltpu.VMEM((GRADIENT_TILES, TILE, TILE), BF16),
        w_odd=pltpu.VMEM((GRADIENT_TILES, TILE, TILE), BF16),
        grad=pltpu.VMEM((blocks, ds, TILE), F32),
    )


def student_phase(starts, spare, x_in, c):
    pack(starts, spare, x_in, c["students"], c["rows"].at[0], c["weights"].at[0], 3)
    sweep(
        STUDENT_TILES, c["rows"].at[0], c["weights"].at[0], c["even"], c["odd"], c["tops"],
        c["running"], c["s_state"], c["s_ref"], None,
    )


def teacher_phase(starts, spare, x_in, c):
    pack(starts, spare, x_in, None, c["rows"].at[1], c["weights"].at[1], 2)
    sweep(
        TEACHER_TILES, c["rows"].at[1], c["weights"].at[1], c["even"], c["odd"], c["tops"],
        c["running"], c["t_state"], c["pt_ref"], c["s_ref"],
    )
    return totals(c["s_state"], c["t_state"], c["stats"])


def gradient_phase(first, last, final, now, c, row_done):
    refs = [c[k] for k in ("students", "s_ref", "pt_ref", "tops", "stats", "grad")]
    if now is None:
        now = chain((jnp.int32(LIVE // TILE - 1), jnp.int32(0)), back, GRADIENT_TILES)
        gradient_step(now, [], c["w_even"], None, *refs)
    return gradients(first, last, final, now, c["w_even"], c["w_odd"], row_done, *refs)


def kernel(
    n, m, counts, t_ref, s_ref, o_ref, loss_ref,
    t_out, s_out, t_in, s_in, c, g_out, g_in, starts, part, row, grid, sems,
):
    x_send, x_recv, g_send, g_recv, seq_send, seq_recv, head_send, head_recv, own = sems
    blocks = LIVE // TILE
    spare = n - blocks
    grad = c["grad"]
    ds = grad.shape[1]
    me, peers = others("seq", n)
    my_head, head_peers = others("head", m)
    barrier = pltpu.get_barrier_semaphore()
    for peer in [{"seq": p} for p in peers] + [{"head": p} for p in head_peers]:
        pl.semaphore_signal(barrier, inc=1, device_id=peer, device_id_type=MESH)

    shift, real = own_start(counts, n)
    turned = turn(shift, TILE)
    enter(s_ref, turned, s_out)
    enter(t_ref, turned, t_out)
    start = jnp.int32(0)
    scalars = []
    for b in range(n):
        starts[b] = start
        scalars.append(start)
        start = start + counts[b]
    grad[...] = jnp.zeros_like(grad)
    pl.semaphore_wait(barrier, n - 1 + m - 1)

    copies = []
    for kind, (src, dst) in enumerate(((s_out, s_in), (t_out, t_in))):
        keep = pltpu.make_async_copy(src.at[me], dst.at[me], own.at[kind])
        keep.start()
        copies.append([
            send(src.at[p], dst.at[me], x_send.at[kind, k], x_recv.at[kind, k], {"seq": p})
            for k, p in enumerate(peers)
        ] + [keep])
    for copy in copies[0]:
        copy.wait()
    student_phase(scalars, spare, s_in, c)
    for copy in copies[1]:
        copy.wait()
    loss = teacher_phase(scalars, spare, t_in, c)
    part[...] = loss[:, :LANES] + loss[:, LANES:]

    def finish_block(b):
        lane = lax.broadcasted_iota(jnp.int32, grad.shape[1:], 1)
        first = starts[b]
        top = blocks - 1
        v = grad[jnp.minimum(b, top)]
        for k in range(1, spare + 1):
            q = jnp.clip(b - k, 0, top)
            v = jnp.where(lane + q * TILE >= first, grad[q], v)
        g_out[b] = v.astype(BF16)

    def to_owner(b):
        @pl.when(b == me)
        def _():
            pltpu.make_async_copy(g_out.at[b], g_in.at[me], own.at[1]).start()

        @pl.when(b != me)
        def _():
            send(g_out.at[b], g_in.at[me], g_send.at[b], g_recv.at[me], {"seq": b})

    def row_done(i):
        @pl.when(i + spare + 1 < n)
        def _():
            to_owner(i + spare + 1)

        finish_block(i + spare)

    trips = blocks * (blocks + 1) // 2 // GRADIENT_TILES
    now = gradient_phase(0, 1, False, None, c, row_done)
    own_part = pltpu.make_async_copy(part, row.at[me], own.at[0])
    own_part.start()
    parts = [
        send(part, row.at[me], seq_send.at[k], seq_recv.at[k], {"seq": p})
        for k, p in enumerate(peers)
    ]
    now = gradient_phase(1, trips - 2, False, now, c, row_done)
    own_part.wait()
    for copy in parts:
        copy.wait()
    own_row = pltpu.make_async_copy(row, grid.at[my_head], own.at[0])
    own_row.start()
    row_copies = [
        send(row, grid.at[my_head], head_send.at[k], head_recv.at[k], {"head": p})
        for k, p in enumerate(head_peers)
    ]
    gradient_phase(trips - 2, trips, True, now, c, row_done)
    for b in range(spare):
        finish_block(b)
    for b in range(spare, -1, -1):
        to_owner(b)
    own_row.wait()
    for copy in row_copies:
        copy.wait()
    whole = jnp.int32(0)
    for b in range(n):
        whole = whole + counts[b]
    loss_ref[...] = jnp.sum(jnp.sum(grid[...], axis=(0, 1)), axis=1, keepdims=True) / (
        H_REL * whole.astype(F32)
    )
    unturned = turn(shift, real)
    pltpu.make_async_copy(g_out.at[me], g_in.at[me], own.at[1]).wait()
    for p in peers:
        pltpu.make_async_remote_copy(
            src_ref=g_out.at[p], dst_ref=g_in.at[p], send_sem=g_send.at[p],
            recv_sem=g_recv.at[p], device_id={"seq": p}, device_id_type=MESH,
        ).wait()
    per = TILE // ds
    for k in range(n // per):
        o_ref[:, k * TILE:(k + 1) * TILE] = ds ** -0.5 * lax.dot_general(
            unturned, g_in[k * per:(k + 1) * per].reshape(TILE, TILE),
            (((1,), (1,)), ((), ())), preferred_element_type=F32,
        )


def local(teacher, student, counts):
    n, m = lax.axis_size("seq"), lax.axis_size("head")
    tokens = teacher.shape[0]
    dt, ds = teacher.shape[1] // n, student.shape[1] // n
    vmem = pl.BlockSpec(memory_space=pltpu.VMEM)
    dma = pltpu.SemaphoreType.DMA
    grad, loss = pl.pallas_call(
        functools.partial(kernel, n, m),
        out_shape=(
            jax.ShapeDtypeStruct((tokens, n * ds), F32),
            jax.ShapeDtypeStruct((1, 1), F32),
        ),
        in_specs=[pl.BlockSpec(memory_space=pltpu.SMEM), vmem, vmem],
        out_specs=(vmem, vmem),
        scratch_shapes=[
            pltpu.VMEM((n, dt, tokens), BF16),
            pltpu.VMEM((n, ds, tokens), BF16),
            pltpu.VMEM((n, dt, tokens), BF16),
            pltpu.VMEM((n, ds, tokens), BF16),
            compute_scratch(dt, ds),
            pltpu.VMEM((n, ds, tokens), BF16),
            pltpu.VMEM((n, ds, tokens), BF16),
            pltpu.SMEM((n,), jnp.int32),
            pltpu.VMEM((1, LANES), F32),
            pltpu.VMEM((n, 1, LANES), F32),
            pltpu.VMEM((m, n, 1, LANES), F32),
            [dma((2, n - 1))] * 2 + [dma((n,))] * 2 + [dma((n - 1,))] * 2
            + [dma((m - 1,))] * 2 + [dma((2,))],
        ],
        compiler_params=pltpu.CompilerParams(
            collective_id=0, has_side_effects=True, vmem_limit_bytes=62 << 20
        ),
    )(counts, teacher, student)
    return grad, loss.reshape(())


def solution(mesh):
    return jax.shard_map(
        local,
        mesh=mesh,
        in_specs=(P("seq", "head"), P("seq", "head"), P()),
        out_specs=(P("seq", "head"), P()),
        check_vma=False,
    )
```

```python
import functools

import jax
import jax.numpy as jnp
from jax import lax
from jax.experimental import pallas as pl
from jax.experimental.pallas import tpu as pltpu
from jax.sharding import PartitionSpec as P

H_REL = 128
LIVE = 3072
DIAGONAL_TILES = 12
LOWER_TILES = 11
GRADIENT_TILES = 13
TILE = 256
LANES = 128
LOG2E = 1.4426950408889634
LN2 = 0.6931471805599453
NEGATIVE = -1e30
MESH = pl.DeviceIdType.MESH
F32 = jnp.float32
BF16 = jnp.bfloat16


def others(axis, n):
    me = lax.axis_index(axis)
    return me, [lax.rem(me + k, n) for k in range(1, n)]


def far_first(ring):
    me = lax.axis_index("seq")
    y, z, core = lax.div(me, 4), lax.div(me, 2) & 1, me & 1
    offsets = [(dy, dz, dc) for dy in range(ring) for dz in range(2) for dc in range(2)]
    offsets.sort(key=lambda o: (-min(o[0], ring - o[0]) - 2 * o[1], o))
    return me, [
        lax.rem(y + dy, ring) * 4 + ((z + dz) & 1) * 2 + ((core + dc) & 1)
        for dy, dz, dc in offsets
        if dy + dz + dc
    ]


def send(src, dst, send_sem, recv_sem, device):
    copy = pltpu.make_async_remote_copy(
        src_ref=src, dst_ref=dst, send_sem=send_sem, recv_sem=recv_sem,
        device_id=device, device_id_type=MESH,
    )
    copy.start()
    return copy


def pieces(x, count):
    out = []
    for k in range(count):
        out.append(x.astype(BF16))
        x = x - out[-1].astype(F32)
    return out


def tile_of(i, j):
    return lax.shift_right_logical(i * (i + 1), 1) + j


def own_start(counts, n):
    me = lax.axis_index("seq")
    start, real = jnp.int32(0), jnp.int32(0)
    for b in range(n):
        start = start + jnp.where(b < me, counts[b], 0)
        real = real + jnp.where(b == me, counts[b], 0)
    return start & (TILE - 1), real


def turn(shift, count):
    row = lax.broadcasted_iota(jnp.int32, (TILE, TILE), 0)
    lane = lax.broadcasted_iota(jnp.int32, (TILE, TILE), 1)
    hit = (lane == ((row + shift) & (TILE - 1))) & (row < count)
    return jnp.where(hit, 1.0, 0.0).astype(BF16)


def enter(x_ref, turned, x_out):
    d = x_out.shape[1]
    for c in range(x_ref.shape[1] // LANES):
        part = lax.dot_general(
            x_ref[:, c * LANES:(c + 1) * LANES], turned, (((0,), (0,)), ((), ())),
            preferred_element_type=F32,
        ).astype(BF16)
        for k in range(LANES // d):
            x_out[c * (LANES // d) + k] = part[k * d:(k + 1) * d]


def pack(starts, spare, x_ref, plain, rows, weights, parts):
    blocks, d, _ = x_ref.shape
    lane = lax.broadcasted_iota(jnp.int32, (d, TILE), 1)
    fill = jnp.zeros((LANES - parts * d, TILE), BF16)
    for c in range(LIVE // TILE):
        v = None
        for b in range(c, min(blocks, c + spare + 1)):
            piece = x_ref[b].astype(F32)
            v = piece if v is None else jnp.where(lane >= starts[b] - c * TILE, piece, v)
        if plain is not None:
            plain[c] = v.astype(BF16)
        rows[c] = jnp.concatenate([v] * (LANES // d), axis=0).T.astype(BF16)
        split = pieces(v * (d ** -0.5 * LOG2E), parts)
        weights[c] = jnp.concatenate(split + [fill] if parts * d < LANES else split, axis=0)


def step(later, now, diagonal, rows, weights, into, source, tops, running, state, keep, other):
    now_at = [tile_of(*c) for c in now]
    now_top = [tops[here] for here in now_at]
    sums = [[jnp.zeros(tops.shape[1:], F32)] * 2 for _ in now]
    made = []
    tallest = [None for _ in later]
    for u in range(max(len(now), len(later))):
        if later:
            i, j = later[u]
            made.append(jnp.dot(rows[j], weights[i], preferred_element_type=F32))
        for g in range(TILE // 8):
            if now:
                v = source[u, g]
                p = jnp.exp2(v - now_top[u])
                sums[u] = [sums[u][0] + p, sums[u][1]]
                if other is None:
                    keep[now_at[u], g] = v
                else:
                    keep[now_at[u], g] = p
                    sums[u][1] = sums[u][1] + p * (v - other[now_at[u], g])
            if later:
                v = made[u][g * 8:(g + 1) * 8]
                if diagonal:
                    row = lax.broadcasted_iota(jnp.int32, v.shape, 0) + g * 8
                    v = jnp.where(row <= lax.broadcasted_iota(jnp.int32, v.shape, 1), v, NEGATIVE)
                into[u, g] = v
                tallest[u] = v if g == 0 else jnp.maximum(tallest[u], v)
    for u, (i, j) in enumerate(later):
        top = jnp.maximum(tallest[u], running[i])
        running[i] = top
        tops[tile_of(i, j)] = top
    for u, (i, _) in enumerate(now):
        less = jnp.exp2(state[i, 0] - now_top[u])
        state[i, 0] = now_top[u]
        state[i, 1] = state[i, 1] * less + sums[u][0]
        if other is not None:
            state[i, 2] = state[i, 2] * less + sums[u][1]


def by_parity(count, even, odd, run):
    @pl.when((count & 1) == 0)
    def _():
        run(even, odd)

    @pl.when((count & 1) == 1)
    def _():
        run(odd, even)


def chain(first, after, count):
    out = [first]
    while len(out) < count:
        out.append(after(*out[-1]))
    return out


def sweep(rows, weights, even, odd, tops, running, state, keep, other):
    blocks = rows.shape[0]
    running[...] = jnp.full(running.shape, NEGATIVE, F32)
    state[:, :1] = jnp.full((blocks, 1, *running.shape[1:]), NEGATIVE, F32)
    state[:, 1:] = jnp.zeros((blocks, state.shape[1] - 1, *running.shape[1:]), F32)

    def run(first, after, tiles, unit, diagonal):
        def one(later, now, into, source):
            step(
                later, now, diagonal, rows, weights, into, source, tops, running, state, keep,
                other,
            )

        def trip(count, now):
            later = chain(after(*now[-1]), after, unit)
            by_parity(count, even, odd, lambda source, into: one(later, now, into, source))
            return later

        now = chain((jnp.int32(first[0]), jnp.int32(first[1])), after, unit)
        one(now, [], even, None)
        trips = tiles // unit - 1
        if trips == 1:
            later = chain(after(*now[-1]), after, unit)
            one(later, now, odd, even)
            now = later
        else:
            now = lax.fori_loop(0, trips, trip, now)
        one([], now, None, odd if trips % 2 else even)

    def below(i, j):
        wrap = j + 1 == i
        return jnp.where(wrap, i + 1, i), jnp.where(wrap, 0, j + 1)

    run((0, 0), lambda i, j: (i + 1, j + 1), blocks, DIAGONAL_TILES, True)
    run((1, 0), below, blocks * (blocks - 1) // 2, LOWER_TILES, False)


def totals(s_state, t_state, stats):
    def collect(state):
        top8 = state[:, 0]
        top = jnp.max(top8, axis=1, keepdims=True)
        less = jnp.exp2(top8 - top)
        return top, [
            jnp.sum(state[:, k] * less, axis=1, keepdims=True) for k in range(1, state.shape[1])
        ]

    s_top, (s_sum,) = collect(s_state)
    t_top, (t_sum, cross) = collect(t_state)
    s_lse = s_top + jnp.log2(s_sum)
    kl = cross / t_sum - (t_top + jnp.log2(t_sum)) + s_lse
    stats[...] = jnp.concatenate([s_lse, t_top, 1.0 / t_sum, s_lse], axis=1)
    return jnp.sum(kl, axis=0) * LN2


def back(i, j):
    wrap = j == i
    return jnp.where(wrap, i - 1, i), jnp.where(wrap, 0, j + 1)


def gradient_step(later, now, into, source, students, s_ref, pt_ref, tops, stats, grad):
    nt = (((1,), (1,)), ((), ()))
    parts = []
    for u in range(max(len(now), len(later))):
        if now:
            i, j = now[u]
            parts.append((
                lax.dot_general(students[i], source[u], nt, preferred_element_type=F32),
                jnp.dot(students[j], source[u], preferred_element_type=F32),
            ))
        if not later:
            continue
        i, j = later[u]
        here = tile_of(i, j)
        s_lse, t_top, t_inv = (stats[i, pl.ds(k, 1), :] for k in range(3))
        t_scale = jnp.exp2(tops[here] - t_top) * t_inv
        for g in range(0, TILE // 8, 2):
            w = jnp.exp2(s_ref[here, g:g + 2] - s_lse) - pt_ref[here, g:g + 2] * t_scale
            into[u, g * 8:g * 8 + 16, :] = w.reshape(16, TILE).astype(BF16)
    for (i, j), (key_grad, query_grad) in zip(now, parts):
        grad[j] += key_grad
        grad[i] += query_grad


def gradients(first, last, final, now, even, odd, row_done, *refs):
    def one(later, now, into, source):
        gradient_step(later, now, into, source, *refs)

    def check(now):
        for i, j in now:
            pl.when(i == j)(functools.partial(row_done, i))

    def trip(count, now):
        later = chain(back(*now[-1]), back, len(now))
        by_parity(count, even, odd, lambda source, into: one(later, now, into, source))
        check(now)
        return later

    now = lax.fori_loop(first, last - final, trip, now)
    if final:
        one([], now, None, odd if (last - 1) % 2 else even)
        check(now)
    return now


def compute_scratch(dt, ds):
    blocks = LIVE // TILE
    tiles = blocks * (blocks + 1) // 2
    groups = TILE // 8
    wide = max(DIAGONAL_TILES, LOWER_TILES)
    return dict(
        students=pltpu.VMEM((blocks, ds, TILE), BF16),
        rows=pltpu.VMEM((2, blocks, TILE, LANES), BF16),
        weights=pltpu.VMEM((2, blocks, LANES, TILE), BF16),
        even=pltpu.VMEM((wide, groups, 8, TILE), F32),
        odd=pltpu.VMEM((wide, groups, 8, TILE), F32),
        s_ref=pltpu.VMEM((tiles, groups, 8, TILE), F32),
        pt_ref=pltpu.VMEM((tiles, groups, 8, TILE), F32),
        tops=pltpu.VMEM((tiles, 8, TILE), F32),
        running=pltpu.VMEM((blocks, 8, TILE), F32),
        s_state=pltpu.VMEM((blocks, 2, 8, TILE), F32),
        t_state=pltpu.VMEM((blocks, 3, 8, TILE), F32),
        stats=pltpu.VMEM((blocks, 4, TILE), F32),
        w_even=pltpu.VMEM((GRADIENT_TILES, TILE, TILE), BF16),
        w_odd=pltpu.VMEM((GRADIENT_TILES, TILE, TILE), BF16),
        grad=pltpu.VMEM((blocks, ds, TILE), F32),
    )


def student_phase(starts, spare, x_in, c):
    pack(starts, spare, x_in, c["students"], c["rows"].at[0], c["weights"].at[0], 3)
    sweep(
        c["rows"].at[0], c["weights"].at[0], c["even"], c["odd"], c["tops"],
        c["running"], c["s_state"], c["s_ref"], None,
    )


def teacher_phase(starts, spare, x_in, c):
    pack(starts, spare, x_in, None, c["rows"].at[1], c["weights"].at[1], 2)
    sweep(
        c["rows"].at[1], c["weights"].at[1], c["even"], c["odd"], c["tops"],
        c["running"], c["t_state"], c["pt_ref"], c["s_ref"],
    )
    return totals(c["s_state"], c["t_state"], c["stats"])


def gradient_phase(first, last, final, now, c, row_done):
    refs = [c[k] for k in ("students", "s_ref", "pt_ref", "tops", "stats", "grad")]
    if now is None:
        now = chain((jnp.int32(LIVE // TILE - 1), jnp.int32(0)), back, GRADIENT_TILES)
        gradient_step(now, [], c["w_even"], None, *refs)
    return gradients(first, last, final, now, c["w_even"], c["w_odd"], row_done, *refs)


def kernel(
    n, m, counts, t_ref, s_ref, o_ref, loss_ref,
    t_own, s_own, t_out, s_out, t_in, s_in, c, g_out, g_in, starts, part, row, grid, sems,
):
    x_send, x_recv, g_send, g_recv, seq_send, seq_recv, head_send, head_recv, own = sems
    blocks = LIVE // TILE
    spare = n - blocks
    grad = c["grad"]
    ds = grad.shape[1]
    me, peers = far_first(n // 4)
    my_head, head_peers = others("head", m)
    barrier = pltpu.get_barrier_semaphore()
    for peer in [{"seq": p} for p in peers] + [{"head": p} for p in head_peers]:
        pl.semaphore_signal(barrier, inc=1, device_id=peer, device_id_type=MESH)

    s_load = pltpu.make_async_copy(s_ref, s_own, own.at[0])
    t_load = pltpu.make_async_copy(t_ref, t_own, own.at[1])
    s_load.start()
    t_load.start()
    shift, real = own_start(counts, n)
    turned = turn(shift, TILE)
    s_load.wait()
    enter(s_own, turned, s_out)
    t_load.wait()
    enter(t_own, turned, t_out)
    start = jnp.int32(0)
    scalars = []
    for b in range(n):
        starts[b] = start
        scalars.append(start)
        start = start + counts[b]
    grad[...] = jnp.zeros_like(grad)
    pl.semaphore_wait(barrier, n - 1 + m - 1)

    copies = []
    for kind, (src, dst) in enumerate(((s_out, s_in), (t_out, t_in))):
        keep = pltpu.make_async_copy(src.at[me], dst.at[me], own.at[kind])
        keep.start()
        copies.append([
            send(src.at[p], dst.at[me], x_send.at[kind, k], x_recv.at[kind, k], {"seq": p})
            for k, p in enumerate(peers)
        ] + [keep])
    for copy in copies[0]:
        copy.wait()
    student_phase(scalars, spare, s_in, c)
    for copy in copies[1]:
        copy.wait()
    loss = teacher_phase(scalars, spare, t_in, c)
    part[...] = loss[:, :LANES] + loss[:, LANES:]

    def finish_block(b):
        lane = lax.broadcasted_iota(jnp.int32, grad.shape[1:], 1)
        first = starts[b]
        top = blocks - 1
        v = grad[jnp.minimum(b, top)]
        for k in range(1, spare + 1):
            q = jnp.clip(b - k, 0, top)
            v = jnp.where(lane + q * TILE >= first, grad[q], v)
        g_out[b] = v.astype(BF16)

    def to_owner(b):
        @pl.when(b == me)
        def _():
            pltpu.make_async_copy(g_out.at[b], g_in.at[me], own.at[1]).start()

        @pl.when(b != me)
        def _():
            send(g_out.at[b], g_in.at[me], g_send.at[b], g_recv.at[me], {"seq": b})

    def row_done(i):
        @pl.when(i + spare + 1 < n)
        def _():
            to_owner(i + spare + 1)

        finish_block(i + spare)

    trips = blocks * (blocks + 1) // 2 // GRADIENT_TILES
    now = gradient_phase(0, 1, False, None, c, row_done)
    own_part = pltpu.make_async_copy(part, row.at[me], own.at[0])
    own_part.start()
    parts = [
        send(part, row.at[me], seq_send.at[k], seq_recv.at[k], {"seq": p})
        for k, p in enumerate(peers)
    ]
    now = gradient_phase(1, trips - 1, False, now, c, row_done)
    own_part.wait()
    for copy in parts:
        copy.wait()
    own_row = pltpu.make_async_copy(row, grid.at[my_head], own.at[0])
    own_row.start()
    row_copies = [
        send(row, grid.at[my_head], head_send.at[k], head_recv.at[k], {"head": p})
        for k, p in enumerate(head_peers)
    ]
    gradient_phase(trips - 1, trips, True, now, c, row_done)
    for b in range(spare):
        finish_block(b)
    for b in range(spare, -1, -1):
        to_owner(b)
    own_row.wait()
    for copy in row_copies:
        copy.wait()
    whole = jnp.int32(0)
    for b in range(n):
        whole = whole + counts[b]
    loss_ref[...] = jnp.sum(jnp.sum(grid[...], axis=(0, 1)), axis=1, keepdims=True) / (
        H_REL * whole.astype(F32)
    )
    unturned = turn(shift, real)
    pltpu.make_async_copy(g_out.at[me], g_in.at[me], own.at[1]).wait()
    for p in peers:
        pltpu.make_async_remote_copy(
            src_ref=g_out.at[p], dst_ref=g_in.at[p], send_sem=g_send.at[p],
            recv_sem=g_recv.at[p], device_id={"seq": p}, device_id_type=MESH,
        ).wait()
    per = TILE // ds
    for k in range(n // per):
        o_ref[:, k * TILE:(k + 1) * TILE] = lax.dot_general(
            unturned, g_in[k * per:(k + 1) * per].reshape(TILE, TILE),
            (((1,), (1,)), ((), ())), preferred_element_type=F32,
        ).astype(BF16)


def local(teacher, student, counts):
    n, m = lax.axis_size("seq"), lax.axis_size("head")
    tokens = teacher.shape[0]
    dt, ds = teacher.shape[1] // n, student.shape[1] // n
    vmem = pl.BlockSpec(memory_space=pltpu.VMEM)
    any_space = pl.BlockSpec(memory_space=pl.ANY)
    dma = pltpu.SemaphoreType.DMA
    grad, loss = pl.pallas_call(
        functools.partial(kernel, n, m),
        out_shape=(
            jax.ShapeDtypeStruct((tokens, n * ds), BF16),
            jax.ShapeDtypeStruct((1, 1), F32),
        ),
        in_specs=[pl.BlockSpec(memory_space=pltpu.SMEM), any_space, any_space],
        out_specs=(vmem, vmem),
        scratch_shapes=[
            pltpu.VMEM(teacher.shape, BF16),
            pltpu.VMEM(student.shape, BF16),
            pltpu.VMEM((n, dt, tokens), BF16),
            pltpu.VMEM((n, ds, tokens), BF16),
            pltpu.VMEM((n, dt, tokens), BF16),
            pltpu.VMEM((n, ds, tokens), BF16),
            compute_scratch(dt, ds),
            pltpu.VMEM((n, ds, tokens), BF16),
            pltpu.VMEM((n, ds, tokens), BF16),
            pltpu.SMEM((n,), jnp.int32),
            pltpu.VMEM((1, LANES), F32),
            pltpu.VMEM((n, 1, LANES), F32),
            pltpu.VMEM((m, n, 1, LANES), F32),
            [dma((2, n - 1))] * 2 + [dma((n,))] * 2 + [dma((n - 1,))] * 2
            + [dma((m - 1,))] * 2 + [dma((2,))],
        ],
        compiler_params=pltpu.CompilerParams(
            collective_id=0, has_side_effects=True, vmem_limit_bytes=62 << 20
        ),
    )(counts, teacher, student)
    return grad.astype(F32) * ds ** -0.5, loss.reshape(())


def solution(mesh):
    return jax.shard_map(
        local,
        mesh=mesh,
        in_specs=(P("seq", "head"), P("seq", "head"), P()),
        out_specs=(P("seq", "head"), P()),
        check_vma=False,
    )
```

```python
import functools

import jax
import jax.numpy as jnp
from jax import lax
from jax.experimental import pallas as pl
from jax.experimental.pallas import tpu as pltpu
from jax.sharding import PartitionSpec as P

H_REL = 128
LIVE = 3072
DIAGONAL_TILES = 12
LOWER_TILES = 11
GRADIENT_TILES = 13
TILE = 256
LANES = 128
LOG2E = 1.4426950408889634
LN2 = 0.6931471805599453
NEGATIVE = -1e30
MESH = pl.DeviceIdType.MESH
F32 = jnp.float32
BF16 = jnp.bfloat16


def others(axis, n):
    me = lax.axis_index(axis)
    return me, [lax.rem(me + k, n) for k in range(1, n)]


def far_first(ring):
    me = lax.axis_index("seq")
    y, z, core = lax.div(me, 4), lax.div(me, 2) & 1, me & 1
    offsets = [(dy, dz, dc) for dy in range(ring) for dz in range(2) for dc in range(2)]
    offsets.sort(key=lambda o: (-min(o[0], ring - o[0]) - 2 * o[1], o))
    return me, [
        lax.rem(y + dy, ring) * 4 + ((z + dz) & 1) * 2 + ((core + dc) & 1)
        for dy, dz, dc in offsets
        if dy + dz + dc
    ]


def send(src, dst, send_sem, recv_sem, device):
    copy = pltpu.make_async_remote_copy(
        src_ref=src, dst_ref=dst, send_sem=send_sem, recv_sem=recv_sem,
        device_id=device, device_id_type=MESH,
    )
    copy.start()
    return copy


def pieces(x, count):
    out = []
    for k in range(count):
        out.append(x.astype(BF16))
        x = x - out[-1].astype(F32)
    return out


def tile_of(i, j):
    return lax.shift_right_logical(i * (i + 1), 1) + j


def own_start(counts, n):
    me = lax.axis_index("seq")
    start, real = jnp.int32(0), jnp.int32(0)
    for b in range(n):
        start = start + jnp.where(b < me, counts[b], 0)
        real = real + jnp.where(b == me, counts[b], 0)
    return start & (TILE - 1), real


def turn(shift, count):
    row = lax.broadcasted_iota(jnp.int32, (TILE, TILE), 0)
    lane = lax.broadcasted_iota(jnp.int32, (TILE, TILE), 1)
    hit = (lane == ((row + shift) & (TILE - 1))) & (row < count)
    return jnp.where(hit, 1.0, 0.0).astype(BF16)


def enter(x_ref, turned, x_out):
    d = x_out.shape[1]
    for c in range(x_ref.shape[1] // LANES):
        part = lax.dot_general(
            x_ref[:, c * LANES:(c + 1) * LANES], turned, (((0,), (0,)), ((), ())),
            preferred_element_type=F32,
        ).astype(BF16)
        for k in range(LANES // d):
            x_out[c * (LANES // d) + k] = part[k * d:(k + 1) * d]


def pack(starts, spare, x_ref, plain, rows, weights, parts):
    blocks, d, _ = x_ref.shape
    lane = lax.broadcasted_iota(jnp.int32, (d, TILE), 1)
    fill = jnp.zeros((LANES - parts * d, TILE), BF16)
    for c in range(LIVE // TILE):
        v = None
        for b in range(c, min(blocks, c + spare + 1)):
            piece = x_ref[b].astype(F32)
            v = piece if v is None else jnp.where(lane >= starts[b] - c * TILE, piece, v)
        if plain is not None:
            plain[c] = v.astype(BF16)
        rows[c] = jnp.concatenate([v] * (LANES // d), axis=0).T.astype(BF16)
        split = pieces(v * (d ** -0.5 * LOG2E), parts)
        weights[c] = jnp.concatenate(split + [fill] if parts * d < LANES else split, axis=0)


def step(later, now, diagonal, rows, weights, into, source, tops, running, state, keep, other):
    now_at = [tile_of(*c) for c in now]
    now_top = [tops[here] for here in now_at]
    sums = [[jnp.zeros(tops.shape[1:], F32)] * 2 for _ in now]
    made = []
    tallest = [None for _ in later]
    for u in range(max(len(now), len(later))):
        if later:
            i, j = later[u]
            made.append(jnp.dot(rows[j], weights[i], preferred_element_type=F32))
        for g in range(TILE // 8):
            if now:
                v = source[u, g]
                p = jnp.exp2(v - now_top[u])
                sums[u] = [sums[u][0] + p, sums[u][1]]
                if other is None:
                    keep[now_at[u], g] = v
                else:
                    keep[now_at[u], g] = p
                    sums[u][1] = sums[u][1] + p * (v - other[now_at[u], g])
            if later:
                v = made[u][g * 8:(g + 1) * 8]
                if diagonal:
                    row = lax.broadcasted_iota(jnp.int32, v.shape, 0) + g * 8
                    v = jnp.where(row <= lax.broadcasted_iota(jnp.int32, v.shape, 1), v, NEGATIVE)
                into[u, g] = v
                tallest[u] = v if g == 0 else jnp.maximum(tallest[u], v)
    for u, (i, j) in enumerate(later):
        top = jnp.maximum(tallest[u], running[i])
        running[i] = top
        tops[tile_of(i, j)] = top
    for u, (i, _) in enumerate(now):
        less = jnp.exp2(state[i, 0] - now_top[u])
        state[i, 0] = now_top[u]
        state[i, 1] = state[i, 1] * less + sums[u][0]
        if other is not None:
            state[i, 2] = state[i, 2] * less + sums[u][1]


def by_parity(count, even, odd, run):
    @pl.when((count & 1) == 0)
    def _():
        run(even, odd)

    @pl.when((count & 1) == 1)
    def _():
        run(odd, even)


def chain(first, after, count):
    out = [first]
    while len(out) < count:
        out.append(after(*out[-1]))
    return out


def sweep(rows, weights, even, odd, tops, running, state, keep, other):
    blocks = rows.shape[0]
    running[...] = jnp.full(running.shape, NEGATIVE, F32)
    state[:, :1] = jnp.full((blocks, 1, *running.shape[1:]), NEGATIVE, F32)
    state[:, 1:] = jnp.zeros((blocks, state.shape[1] - 1, *running.shape[1:]), F32)

    def run(first, after, tiles, unit, diagonal):
        def one(later, now, into, source):
            step(
                later, now, diagonal, rows, weights, into, source, tops, running, state, keep,
                other,
            )

        def trip(count, now):
            later = chain(after(*now[-1]), after, unit)
            by_parity(count, even, odd, lambda source, into: one(later, now, into, source))
            return later

        now = chain((jnp.int32(first[0]), jnp.int32(first[1])), after, unit)
        one(now, [], even, None)
        trips = tiles // unit - 1
        if trips == 1:
            later = chain(after(*now[-1]), after, unit)
            one(later, now, odd, even)
            now = later
        else:
            now = lax.fori_loop(0, trips, trip, now)
        one([], now, None, odd if trips % 2 else even)

    def below(i, j):
        wrap = j + 1 == i
        return jnp.where(wrap, i + 1, i), jnp.where(wrap, 0, j + 1)

    run((0, 0), lambda i, j: (i + 1, j + 1), blocks, DIAGONAL_TILES, True)
    run((1, 0), below, blocks * (blocks - 1) // 2, LOWER_TILES, False)


def totals(s_state, t_state, stats):
    def collect(state):
        top8 = state[:, 0]
        top = jnp.max(top8, axis=1, keepdims=True)
        less = jnp.exp2(top8 - top)
        return top, [
            jnp.sum(state[:, k] * less, axis=1, keepdims=True) for k in range(1, state.shape[1])
        ]

    s_top, (s_sum,) = collect(s_state)
    t_top, (t_sum, cross) = collect(t_state)
    s_lse = s_top + jnp.log2(s_sum)
    kl = cross / t_sum - (t_top + jnp.log2(t_sum)) + s_lse
    stats[...] = jnp.concatenate([s_lse, t_top, 1.0 / t_sum, s_lse], axis=1)
    return jnp.sum(kl, axis=0) * LN2


def back(i, j):
    wrap = j == i
    return jnp.where(wrap, i - 1, i), jnp.where(wrap, 0, j + 1)


def gradient_step(later, now, into, source, students, s_ref, pt_ref, tops, stats, grad):
    nt = (((1,), (1,)), ((), ()))
    parts = []
    for u in range(max(len(now), len(later))):
        if now:
            i, j = now[u]
            parts.append((
                lax.dot_general(students[i], source[u], nt, preferred_element_type=F32),
                jnp.dot(students[j], source[u], preferred_element_type=F32),
            ))
        if not later:
            continue
        i, j = later[u]
        here = tile_of(i, j)
        s_lse, t_top, t_inv = (stats[i, pl.ds(k, 1), :] for k in range(3))
        t_scale = jnp.exp2(tops[here] - t_top) * t_inv
        for g in range(0, TILE // 8, 2):
            w = jnp.exp2(s_ref[here, g:g + 2] - s_lse) - pt_ref[here, g:g + 2] * t_scale
            into[u, g * 8:g * 8 + 16, :] = w.reshape(16, TILE).astype(BF16)
    for (i, j), (key_grad, query_grad) in zip(now, parts):
        grad[j] += key_grad
        grad[i] += query_grad


def gradients(first, last, final, now, even, odd, row_done, *refs):
    def one(later, now, into, source):
        gradient_step(later, now, into, source, *refs)

    def check(now):
        for i, j in now:
            pl.when(i == j)(functools.partial(row_done, i))

    def trip(count, now):
        later = chain(back(*now[-1]), back, len(now))
        by_parity(count, even, odd, lambda source, into: one(later, now, into, source))
        check(now)
        return later

    now = lax.fori_loop(first, last - final, trip, now)
    if final:
        one([], now, None, odd if (last - 1) % 2 else even)
        check(now)
    return now


def compute_scratch(dt, ds):
    blocks = LIVE // TILE
    tiles = blocks * (blocks + 1) // 2
    groups = TILE // 8
    wide = max(DIAGONAL_TILES, LOWER_TILES)
    return dict(
        students=pltpu.VMEM((blocks, ds, TILE), BF16),
        rows=pltpu.VMEM((2, blocks, TILE, LANES), BF16),
        weights=pltpu.VMEM((2, blocks, LANES, TILE), BF16),
        even=pltpu.VMEM((wide, groups, 8, TILE), F32),
        odd=pltpu.VMEM((wide, groups, 8, TILE), F32),
        s_ref=pltpu.VMEM((tiles, groups, 8, TILE), F32),
        pt_ref=pltpu.VMEM((tiles, groups, 8, TILE), F32),
        tops=pltpu.VMEM((tiles, 8, TILE), F32),
        running=pltpu.VMEM((blocks, 8, TILE), F32),
        s_state=pltpu.VMEM((blocks, 2, 8, TILE), F32),
        t_state=pltpu.VMEM((blocks, 3, 8, TILE), F32),
        stats=pltpu.VMEM((blocks, 4, TILE), F32),
        w_even=pltpu.VMEM((GRADIENT_TILES, TILE, TILE), BF16),
        w_odd=pltpu.VMEM((GRADIENT_TILES, TILE, TILE), BF16),
        grad=pltpu.VMEM((blocks, ds, TILE), F32),
    )


def student_phase(starts, spare, x_in, c):
    pack(starts, spare, x_in, c["students"], c["rows"].at[0], c["weights"].at[0], 3)
    sweep(
        c["rows"].at[0], c["weights"].at[0], c["even"], c["odd"], c["tops"],
        c["running"], c["s_state"], c["s_ref"], None,
    )


def teacher_phase(starts, spare, x_in, c):
    pack(starts, spare, x_in, None, c["rows"].at[1], c["weights"].at[1], 2)
    sweep(
        c["rows"].at[1], c["weights"].at[1], c["even"], c["odd"], c["tops"],
        c["running"], c["t_state"], c["pt_ref"], c["s_ref"],
    )
    return totals(c["s_state"], c["t_state"], c["stats"])


def gradient_phase(first, last, final, now, c, row_done):
    refs = [c[k] for k in ("students", "s_ref", "pt_ref", "tops", "stats", "grad")]
    if now is None:
        now = chain((jnp.int32(LIVE // TILE - 1), jnp.int32(0)), back, GRADIENT_TILES)
        gradient_step(now, [], c["w_even"], None, *refs)
    return gradients(first, last, final, now, c["w_even"], c["w_odd"], row_done, *refs)


def kernel(
    n, m, counts, t_ref, s_ref, g_in, loss_ref,
    t_own, s_own, t_out, s_out, t_in, s_in, c, g_out, starts, part, row, grid, sems,
):
    x_send, x_recv, g_send, g_recv, seq_send, seq_recv, head_send, head_recv, own = sems
    blocks = LIVE // TILE
    spare = n - blocks
    grad = c["grad"]
    ds = grad.shape[1]
    me, peers = far_first(n // 4)
    my_head, head_peers = others("head", m)
    barrier = pltpu.get_barrier_semaphore()
    for peer in [{"seq": p} for p in peers] + [{"head": p} for p in head_peers]:
        pl.semaphore_signal(barrier, inc=1, device_id=peer, device_id_type=MESH)

    s_load = pltpu.make_async_copy(s_ref, s_own, own.at[0])
    t_load = pltpu.make_async_copy(t_ref, t_own, own.at[1])
    s_load.start()
    t_load.start()
    shift, _ = own_start(counts, n)
    turned = turn(shift, TILE)
    s_load.wait()
    enter(s_own, turned, s_out)
    t_load.wait()
    enter(t_own, turned, t_out)
    start = jnp.int32(0)
    scalars = []
    for b in range(n):
        starts[b] = start
        scalars.append(start)
        start = start + counts[b]
    grad[...] = jnp.zeros_like(grad)
    pl.semaphore_wait(barrier, n - 1 + m - 1)

    copies = []
    for kind, (src, dst) in enumerate(((s_out, s_in), (t_out, t_in))):
        keep = pltpu.make_async_copy(src.at[me], dst.at[me], own.at[kind])
        keep.start()
        copies.append([
            send(src.at[p], dst.at[me], x_send.at[kind, k], x_recv.at[kind, k], {"seq": p})
            for k, p in enumerate(peers)
        ] + [keep])
    for copy in copies[0]:
        copy.wait()
    student_phase(scalars, spare, s_in, c)
    for copy in copies[1]:
        copy.wait()
    loss = teacher_phase(scalars, spare, t_in, c)
    part[...] = loss[:, :LANES] + loss[:, LANES:]

    def finish_block(b):
        lane = lax.broadcasted_iota(jnp.int32, grad.shape[1:], 1)
        first = starts[b]
        top = blocks - 1
        v = grad[jnp.minimum(b, top)]
        for k in range(1, spare + 1):
            q = jnp.clip(b - k, 0, top)
            v = jnp.where(lane + q * TILE >= first, grad[q], v)
        g_out[b] = v.astype(BF16)

    def to_owner(b):
        @pl.when(b == me)
        def _():
            pltpu.make_async_copy(g_out.at[b], g_in.at[me], own.at[1]).start()

        @pl.when(b != me)
        def _():
            send(g_out.at[b], g_in.at[me], g_send.at[b], g_recv.at[me], {"seq": b})

    def row_done(i):
        @pl.when(i + spare + 1 < n)
        def _():
            to_owner(i + spare + 1)

        finish_block(i + spare)

    trips = blocks * (blocks + 1) // 2 // GRADIENT_TILES
    now = gradient_phase(0, 0, False, None, c, row_done)
    own_part = pltpu.make_async_copy(part, row.at[me], own.at[0])
    own_part.start()
    parts = [
        send(part, row.at[me], seq_send.at[k], seq_recv.at[k], {"seq": p})
        for k, p in enumerate(peers)
    ]
    now = gradient_phase(0, trips - 1, False, now, c, row_done)
    own_part.wait()
    for copy in parts:
        copy.wait()
    own_row = pltpu.make_async_copy(row, grid.at[my_head], own.at[0])
    own_row.start()
    row_copies = [
        send(row, grid.at[my_head], head_send.at[k], head_recv.at[k], {"head": p})
        for k, p in enumerate(head_peers)
    ]
    gradient_phase(trips - 1, trips, True, now, c, row_done)
    for b in range(spare):
        finish_block(b)
    for b in range(spare, -1, -1):
        to_owner(b)
    own_row.wait()
    for copy in row_copies:
        copy.wait()
    whole = jnp.int32(0)
    for b in range(n):
        whole = whole + counts[b]
    loss_ref[...] = jnp.sum(jnp.sum(grid[...], axis=(0, 1)), axis=1, keepdims=True) / (
        H_REL * whole.astype(F32)
    )
    pltpu.make_async_copy(g_out.at[me], g_in.at[me], own.at[1]).wait()
    for p in peers:
        pltpu.make_async_remote_copy(
            src_ref=g_out.at[p], dst_ref=g_in.at[p], send_sem=g_send.at[p],
            recv_sem=g_recv.at[p], device_id={"seq": p}, device_id_type=MESH,
        ).wait()


def leave_kernel(n, counts, g_ref, o_ref):
    ds = g_ref.shape[1]
    per = TILE // ds
    turned = turn(*own_start(counts, n))
    for k in range(n // per):
        o_ref[:, k * TILE:(k + 1) * TILE] = ds ** -0.5 * lax.dot_general(
            turned, g_ref[k * per:(k + 1) * per].reshape(TILE, TILE),
            (((1,), (1,)), ((), ())), preferred_element_type=F32,
        )


def local(teacher, student, counts):
    n, m = lax.axis_size("seq"), lax.axis_size("head")
    tokens = teacher.shape[0]
    dt, ds = teacher.shape[1] // n, student.shape[1] // n
    vmem = pl.BlockSpec(memory_space=pltpu.VMEM)
    any_space = pl.BlockSpec(memory_space=pl.ANY)
    smem = pl.BlockSpec(memory_space=pltpu.SMEM)
    dma = pltpu.SemaphoreType.DMA
    grad, loss = pl.pallas_call(
        functools.partial(kernel, n, m),
        out_shape=(
            jax.ShapeDtypeStruct((n, ds, tokens), BF16),
            jax.ShapeDtypeStruct((1, 1), F32),
        ),
        in_specs=[smem, any_space, any_space],
        out_specs=(any_space, vmem),
        scratch_shapes=[
            pltpu.VMEM(teacher.shape, BF16),
            pltpu.VMEM(student.shape, BF16),
            pltpu.VMEM((n, dt, tokens), BF16),
            pltpu.VMEM((n, ds, tokens), BF16),
            pltpu.VMEM((n, dt, tokens), BF16),
            pltpu.VMEM((n, ds, tokens), BF16),
            compute_scratch(dt, ds),
            pltpu.VMEM((n, ds, tokens), BF16),
            pltpu.SMEM((n,), jnp.int32),
            pltpu.VMEM((1, LANES), F32),
            pltpu.VMEM((n, 1, LANES), F32),
            pltpu.VMEM((m, n, 1, LANES), F32),
            [dma((2, n - 1))] * 2 + [dma((n,))] * 2 + [dma((n - 1,))] * 2
            + [dma((m - 1,))] * 2 + [dma((2,))],
        ],
        compiler_params=pltpu.CompilerParams(
            collective_id=0, has_side_effects=True, vmem_limit_bytes=62 << 20
        ),
    )(counts, teacher, student)
    grad = pl.pallas_call(
        functools.partial(leave_kernel, n),
        out_shape=jax.ShapeDtypeStruct((tokens, n * ds), F32),
        in_specs=[smem, vmem],
        out_specs=vmem,
    )(counts, grad)
    return grad, loss.reshape(())


def solution(mesh):
    return jax.shard_map(
        local,
        mesh=mesh,
        in_specs=(P("seq", "head"), P("seq", "head"), P()),
        out_specs=(P("seq", "head"), P()),
        check_vma=False,
    )
```

```python
import functools

import jax
import jax.numpy as jnp
from jax import lax
from jax.experimental import pallas as pl
from jax.experimental.pallas import tpu as pltpu
from jax.sharding import PartitionSpec as P

H_REL = 128
LIVE = 3072
DIAGONAL_TILES = 12
LOWER_TILES = 11
GRADIENT_TILES = 13
TILE = 256
LANES = 128
LOG2E = 1.4426950408889634
LN2 = 0.6931471805599453
NEGATIVE = -1e30
MESH = pl.DeviceIdType.MESH
F32 = jnp.float32
BF16 = jnp.bfloat16


def others(axis, n):
    me = lax.axis_index(axis)
    return me, [lax.rem(me + k, n) for k in range(1, n)]


def far_first(ring):
    me = lax.axis_index("seq")
    y, z, core = lax.div(me, 4), lax.div(me, 2) & 1, me & 1
    offsets = [(dy, dz, dc) for dy in range(ring) for dz in range(2) for dc in range(2)]
    offsets.sort(key=lambda o: (-min(o[0], ring - o[0]) - 2 * o[1], o))
    return me, [
        lax.rem(y + dy, ring) * 4 + ((z + dz) & 1) * 2 + ((core + dc) & 1)
        for dy, dz, dc in offsets
        if dy + dz + dc
    ]


def send(src, dst, send_sem, recv_sem, device):
    copy = pltpu.make_async_remote_copy(
        src_ref=src, dst_ref=dst, send_sem=send_sem, recv_sem=recv_sem,
        device_id=device, device_id_type=MESH,
    )
    copy.start()
    return copy


def pieces(x, count):
    out = []
    for k in range(count):
        out.append(x.astype(BF16))
        x = x - out[-1].astype(F32)
    return out


def tile_of(i, j):
    return lax.shift_right_logical(i * (i + 1), 1) + j


def own_start(counts, n):
    me = lax.axis_index("seq")
    start, real = jnp.int32(0), jnp.int32(0)
    for b in range(n):
        start = start + jnp.where(b < me, counts[b], 0)
        real = real + jnp.where(b == me, counts[b], 0)
    return start & (TILE - 1), real


def turn(shift, count):
    row = lax.broadcasted_iota(jnp.int32, (TILE, TILE), 0)
    lane = lax.broadcasted_iota(jnp.int32, (TILE, TILE), 1)
    hit = (lane == ((row + shift) & (TILE - 1))) & (row < count)
    return jnp.where(hit, 1.0, 0.0).astype(BF16)


def enter(x_ref, turned, x_out):
    d = x_out.shape[1]
    for c in range(x_ref.shape[1] // LANES):
        part = lax.dot_general(
            x_ref[:, c * LANES:(c + 1) * LANES], turned, (((0,), (0,)), ((), ())),
            preferred_element_type=F32,
        ).astype(BF16)
        for k in range(LANES // d):
            x_out[c * (LANES // d) + k] = part[k * d:(k + 1) * d]


def pack(starts, spare, x_ref, plain, rows, weights, parts):
    blocks, d, _ = x_ref.shape
    lane = lax.broadcasted_iota(jnp.int32, (d, TILE), 1)
    fill = jnp.zeros((LANES - parts * d, TILE), BF16)
    for c in range(LIVE // TILE):
        v = None
        for b in range(c, min(blocks, c + spare + 1)):
            piece = x_ref[b].astype(F32)
            v = piece if v is None else jnp.where(lane >= starts[b] - c * TILE, piece, v)
        if plain is not None:
            plain[c] = v.astype(BF16)
        rows[c] = jnp.concatenate([v] * (LANES // d), axis=0).T.astype(BF16)
        split = pieces(v * (d ** -0.5 * LOG2E), parts)
        weights[c] = jnp.concatenate(split + [fill] if parts * d < LANES else split, axis=0)


def step(later, now, diagonal, rows, weights, into, source, tops, running, state, keep, other):
    now_at = [tile_of(*c) for c in now]
    now_top = [tops[here] for here in now_at]
    sums = [[jnp.zeros(tops.shape[1:], F32)] * 2 for _ in now]
    made = []
    tallest = [None for _ in later]
    for u in range(max(len(now), len(later))):
        if later:
            i, j = later[u]
            made.append(jnp.dot(rows[j], weights[i], preferred_element_type=F32))
        for g in range(TILE // 8):
            if now:
                v = source[u, g]
                p = jnp.exp2(v - now_top[u])
                sums[u] = [sums[u][0] + p, sums[u][1]]
                if other is None:
                    keep[now_at[u], g] = v
                else:
                    keep[now_at[u], g] = p
                    sums[u][1] = sums[u][1] + p * (v - other[now_at[u], g])
            if later:
                v = made[u][g * 8:(g + 1) * 8]
                if diagonal:
                    row = lax.broadcasted_iota(jnp.int32, v.shape, 0) + g * 8
                    v = jnp.where(row <= lax.broadcasted_iota(jnp.int32, v.shape, 1), v, NEGATIVE)
                into[u, g] = v
                tallest[u] = v if g == 0 else jnp.maximum(tallest[u], v)
    for u, (i, j) in enumerate(later):
        top = jnp.maximum(tallest[u], running[i])
        running[i] = top
        tops[tile_of(i, j)] = top
    for u, (i, _) in enumerate(now):
        less = jnp.exp2(state[i, 0] - now_top[u])
        state[i, 0] = now_top[u]
        state[i, 1] = state[i, 1] * less + sums[u][0]
        if other is not None:
            state[i, 2] = state[i, 2] * less + sums[u][1]


def by_parity(count, even, odd, run):
    @pl.when((count & 1) == 0)
    def _():
        run(even, odd)

    @pl.when((count & 1) == 1)
    def _():
        run(odd, even)


def chain(first, after, count):
    out = [first]
    while len(out) < count:
        out.append(after(*out[-1]))
    return out


def sweep(rows, weights, even, odd, tops, running, state, keep, other):
    blocks = rows.shape[0]
    running[...] = jnp.full(running.shape, NEGATIVE, F32)
    state[:, :1] = jnp.full((blocks, 1, *running.shape[1:]), NEGATIVE, F32)
    state[:, 1:] = jnp.zeros((blocks, state.shape[1] - 1, *running.shape[1:]), F32)

    def run(first, after, tiles, unit, diagonal):
        def one(later, now, into, source):
            step(
                later, now, diagonal, rows, weights, into, source, tops, running, state, keep,
                other,
            )

        def trip(count, now):
            later = chain(after(*now[-1]), after, unit)
            by_parity(count, even, odd, lambda source, into: one(later, now, into, source))
            return later

        now = chain((jnp.int32(first[0]), jnp.int32(first[1])), after, unit)
        one(now, [], even, None)
        trips = tiles // unit - 1
        if trips == 1:
            later = chain(after(*now[-1]), after, unit)
            one(later, now, odd, even)
            now = later
        else:
            now = lax.fori_loop(0, trips, trip, now)
        one([], now, None, odd if trips % 2 else even)

    def below(i, j):
        wrap = j + 1 == i
        return jnp.where(wrap, i + 1, i), jnp.where(wrap, 0, j + 1)

    run((0, 0), lambda i, j: (i + 1, j + 1), blocks, DIAGONAL_TILES, True)
    run((1, 0), below, blocks * (blocks - 1) // 2, LOWER_TILES, False)


def totals(s_state, t_state, stats):
    def collect(state):
        top8 = state[:, 0]
        top = jnp.max(top8, axis=1, keepdims=True)
        less = jnp.exp2(top8 - top)
        return top, [
            jnp.sum(state[:, k] * less, axis=1, keepdims=True) for k in range(1, state.shape[1])
        ]

    s_top, (s_sum,) = collect(s_state)
    t_top, (t_sum, cross) = collect(t_state)
    s_lse = s_top + jnp.log2(s_sum)
    kl = cross / t_sum - (t_top + jnp.log2(t_sum)) + s_lse
    stats[...] = jnp.concatenate([s_lse, t_top, 1.0 / t_sum, s_lse], axis=1)
    return jnp.sum(kl, axis=0) * LN2


def back(i, j):
    wrap = j == i
    return jnp.where(wrap, i - 1, i), jnp.where(wrap, 0, j + 1)


def gradient_step(later, now, into, source, students, s_ref, pt_ref, tops, stats, grad):
    nt = (((1,), (1,)), ((), ()))
    parts = []
    for u in range(max(len(now), len(later))):
        if now:
            i, j = now[u]
            parts.append((
                lax.dot_general(students[i], source[u], nt, preferred_element_type=F32),
                jnp.dot(students[j], source[u], preferred_element_type=F32),
            ))
        if not later:
            continue
        i, j = later[u]
        here = tile_of(i, j)
        s_lse, t_top, t_inv = (stats[i, pl.ds(k, 1), :] for k in range(3))
        t_scale = jnp.exp2(tops[here] - t_top) * t_inv
        for g in range(0, TILE // 8, 2):
            w = jnp.exp2(s_ref[here, g:g + 2] - s_lse) - pt_ref[here, g:g + 2] * t_scale
            into[u, g * 8:g * 8 + 16, :] = w.reshape(16, TILE).astype(BF16)
    for (i, j), (key_grad, query_grad) in zip(now, parts):
        grad[j] += key_grad
        grad[i] += query_grad


def gradients(first, last, final, now, even, odd, row_done, *refs):
    def one(later, now, into, source):
        gradient_step(later, now, into, source, *refs)

    def check(now):
        for i, j in now:
            pl.when(i == j)(functools.partial(row_done, i))

    def trip(count, now):
        later = chain(back(*now[-1]), back, len(now))
        by_parity(count, even, odd, lambda source, into: one(later, now, into, source))
        check(now)
        return later

    now = lax.fori_loop(first, last - final, trip, now)
    if final:
        one([], now, None, odd if (last - 1) % 2 else even)
        check(now)
    return now


def compute_scratch(dt, ds):
    blocks = LIVE // TILE
    tiles = blocks * (blocks + 1) // 2
    groups = TILE // 8
    wide = max(DIAGONAL_TILES, LOWER_TILES)
    return dict(
        students=pltpu.VMEM((blocks, ds, TILE), BF16),
        rows=pltpu.VMEM((2, blocks, TILE, LANES), BF16),
        weights=pltpu.VMEM((2, blocks, LANES, TILE), BF16),
        even=pltpu.VMEM((wide, groups, 8, TILE), F32),
        odd=pltpu.VMEM((wide, groups, 8, TILE), F32),
        s_ref=pltpu.VMEM((tiles, groups, 8, TILE), F32),
        pt_ref=pltpu.VMEM((tiles, groups, 8, TILE), F32),
        tops=pltpu.VMEM((tiles, 8, TILE), F32),
        running=pltpu.VMEM((blocks, 8, TILE), F32),
        s_state=pltpu.VMEM((blocks, 2, 8, TILE), F32),
        t_state=pltpu.VMEM((blocks, 3, 8, TILE), F32),
        stats=pltpu.VMEM((blocks, 4, TILE), F32),
        w_even=pltpu.VMEM((GRADIENT_TILES, TILE, TILE), BF16),
        w_odd=pltpu.VMEM((GRADIENT_TILES, TILE, TILE), BF16),
        grad=pltpu.VMEM((blocks, ds, TILE), F32),
    )


def student_phase(starts, spare, x_in, c):
    pack(starts, spare, x_in, c["students"], c["rows"].at[0], c["weights"].at[0], 3)
    sweep(
        c["rows"].at[0], c["weights"].at[0], c["even"], c["odd"], c["tops"],
        c["running"], c["s_state"], c["s_ref"], None,
    )


def teacher_phase(starts, spare, x_in, c):
    pack(starts, spare, x_in, None, c["rows"].at[1], c["weights"].at[1], 2)
    sweep(
        c["rows"].at[1], c["weights"].at[1], c["even"], c["odd"], c["tops"],
        c["running"], c["t_state"], c["pt_ref"], c["s_ref"],
    )
    return totals(c["s_state"], c["t_state"], c["stats"])


def gradient_phase(first, last, final, now, c, row_done):
    refs = [c[k] for k in ("students", "s_ref", "pt_ref", "tops", "stats", "grad")]
    if now is None:
        now = chain((jnp.int32(LIVE // TILE - 1), jnp.int32(0)), back, GRADIENT_TILES)
        gradient_step(now, [], c["w_even"], None, *refs)
    return gradients(first, last, final, now, c["w_even"], c["w_odd"], row_done, *refs)


def kernel(
    n, m, counts, t_ref, s_ref, g_in, loss_ref,
    t_own, s_own, t_out, s_out, t_in, s_in, c, g_out, starts, part, row, grid, sems,
):
    x_send, x_recv, g_send, g_recv, seq_send, seq_recv, head_send, head_recv, own = sems
    blocks = LIVE // TILE
    spare = n - blocks
    grad = c["grad"]
    ds = grad.shape[1]
    me, peers = far_first(n // 4)
    my_head, head_peers = others("head", m)
    barrier = pltpu.get_barrier_semaphore()
    for peer in [{"seq": p} for p in peers] + [{"head": p} for p in head_peers]:
        pl.semaphore_signal(barrier, inc=1, device_id=peer, device_id_type=MESH)

    s_load = pltpu.make_async_copy(s_ref, s_own, own.at[0])
    t_load = pltpu.make_async_copy(t_ref, t_own, own.at[1])
    s_load.start()
    t_load.start()
    shift, _ = own_start(counts, n)
    turned = turn(shift, TILE)
    s_load.wait()
    enter(s_own, turned, s_out)
    t_load.wait()
    enter(t_own, turned, t_out)
    start = jnp.int32(0)
    scalars = []
    for b in range(n):
        starts[b] = start
        scalars.append(start)
        start = start + counts[b]
    grad[...] = jnp.zeros_like(grad)
    pl.semaphore_wait(barrier, n - 1 + m - 1)

    copies, keeps = [], []
    for kind, (src, dst) in enumerate(((s_out, s_in), (t_out, t_in))):
        for copy in copies[0] if kind else []:
            copy.wait_send()
        keeps.append(pltpu.make_async_copy(src.at[me], dst.at[me], own.at[kind]))
        keeps[kind].start()
        copies.append([
            send(src.at[p], dst.at[me], x_send.at[kind, k], x_recv.at[kind, k], {"seq": p})
            for k, p in enumerate(peers)
        ])
    keeps[0].wait()
    for copy in copies[0]:
        copy.wait_recv()
    student_phase(scalars, spare, s_in, c)
    keeps[1].wait()
    for copy in copies[1]:
        copy.wait()
    loss = teacher_phase(scalars, spare, t_in, c)
    part[...] = loss[:, :LANES] + loss[:, LANES:]

    def finish_block(b):
        lane = lax.broadcasted_iota(jnp.int32, grad.shape[1:], 1)
        first = starts[b]
        top = blocks - 1
        v = grad[jnp.minimum(b, top)]
        for k in range(1, spare + 1):
            q = jnp.clip(b - k, 0, top)
            v = jnp.where(lane + q * TILE >= first, grad[q], v)
        g_out[b] = v.astype(BF16)

    def to_owner(b):
        @pl.when(b == me)
        def _():
            pltpu.make_async_copy(g_out.at[b], g_in.at[me], own.at[1]).start()

        @pl.when(b != me)
        def _():
            send(g_out.at[b], g_in.at[me], g_send.at[b], g_recv.at[me], {"seq": b})

    def row_done(i):
        @pl.when(i + spare + 1 < n)
        def _():
            to_owner(i + spare + 1)

        finish_block(i + spare)

    trips = blocks * (blocks + 1) // 2 // GRADIENT_TILES
    now = gradient_phase(0, 0, False, None, c, row_done)
    own_part = pltpu.make_async_copy(part, row.at[me], own.at[0])
    own_part.start()
    parts = [
        send(part, row.at[me], seq_send.at[k], seq_recv.at[k], {"seq": p})
        for k, p in enumerate(peers)
    ]
    now = gradient_phase(0, trips - 1, False, now, c, row_done)
    own_part.wait()
    for copy in parts:
        copy.wait()
    own_row = pltpu.make_async_copy(row, grid.at[my_head], own.at[0])
    own_row.start()
    row_copies = [
        send(row, grid.at[my_head], head_send.at[k], head_recv.at[k], {"head": p})
        for k, p in enumerate(head_peers)
    ]
    gradient_phase(trips - 1, trips, True, now, c, row_done)
    for b in range(spare):
        finish_block(b)
    for b in range(spare, -1, -1):
        to_owner(b)
    own_row.wait()
    for copy in row_copies:
        copy.wait()
    whole = jnp.int32(0)
    for b in range(n):
        whole = whole + counts[b]
    loss_ref[...] = jnp.sum(jnp.sum(grid[...], axis=(0, 1)), axis=1, keepdims=True) / (
        H_REL * whole.astype(F32)
    )
    pltpu.make_async_copy(g_out.at[me], g_in.at[me], own.at[1]).wait()
    for p in peers:
        pltpu.make_async_remote_copy(
            src_ref=g_out.at[p], dst_ref=g_in.at[p], send_sem=g_send.at[p],
            recv_sem=g_recv.at[p], device_id={"seq": p}, device_id_type=MESH,
        ).wait()


def leave_kernel(n, counts, g_ref, o_ref):
    ds = g_ref.shape[1]
    per = TILE // ds
    turned = turn(*own_start(counts, n))
    for k in range(n // per):
        o_ref[:, k * TILE:(k + 1) * TILE] = ds ** -0.5 * lax.dot_general(
            turned, g_ref[k * per:(k + 1) * per].reshape(TILE, TILE),
            (((1,), (1,)), ((), ())), preferred_element_type=F32,
        )


def local(teacher, student, counts):
    n, m = lax.axis_size("seq"), lax.axis_size("head")
    tokens = teacher.shape[0]
    dt, ds = teacher.shape[1] // n, student.shape[1] // n
    vmem = pl.BlockSpec(memory_space=pltpu.VMEM)
    any_space = pl.BlockSpec(memory_space=pl.ANY)
    smem = pl.BlockSpec(memory_space=pltpu.SMEM)
    dma = pltpu.SemaphoreType.DMA
    grad, loss = pl.pallas_call(
        functools.partial(kernel, n, m),
        out_shape=(
            jax.ShapeDtypeStruct((n, ds, tokens), BF16),
            jax.ShapeDtypeStruct((1, 1), F32),
        ),
        in_specs=[smem, any_space, any_space],
        out_specs=(any_space, vmem),
        scratch_shapes=[
            pltpu.VMEM(teacher.shape, BF16),
            pltpu.VMEM(student.shape, BF16),
            pltpu.VMEM((n, dt, tokens), BF16),
            pltpu.VMEM((n, ds, tokens), BF16),
            pltpu.VMEM((n, dt, tokens), BF16),
            pltpu.VMEM((n, ds, tokens), BF16),
            compute_scratch(dt, ds),
            pltpu.VMEM((n, ds, tokens), BF16),
            pltpu.SMEM((n,), jnp.int32),
            pltpu.VMEM((1, LANES), F32),
            pltpu.VMEM((n, 1, LANES), F32),
            pltpu.VMEM((m, n, 1, LANES), F32),
            [dma((2, n - 1))] * 2 + [dma((n,))] * 2 + [dma((n - 1,))] * 2
            + [dma((m - 1,))] * 2 + [dma((2,))],
        ],
        compiler_params=pltpu.CompilerParams(
            collective_id=0, has_side_effects=True, vmem_limit_bytes=62 << 20
        ),
    )(counts, teacher, student)
    grad = pl.pallas_call(
        functools.partial(leave_kernel, n),
        out_shape=jax.ShapeDtypeStruct((tokens, n * ds), F32),
        in_specs=[smem, vmem],
        out_specs=vmem,
    )(counts, grad)
    return grad, loss.reshape(())


def solution(mesh):
    return jax.shard_map(
        local,
        mesh=mesh,
        in_specs=(P("seq", "head"), P("seq", "head"), P()),
        out_specs=(P("seq", "head"), P()),
        check_vma=False,
    )
```

```python
import functools

import jax
import jax.numpy as jnp
from jax import lax
from jax.experimental import pallas as pl
from jax.experimental.pallas import tpu as pltpu
from jax.sharding import PartitionSpec as P

H_REL = 128
LIVE = 3072
DIAGONAL_TILES = 12
LOWER_TILES = 11
GRADIENT_TILES = 13
TILE = 256
LANES = 128
LOG2E = 1.4426950408889634
LN2 = 0.6931471805599453
NEGATIVE = -1e30
MESH = pl.DeviceIdType.MESH
F32 = jnp.float32
BF16 = jnp.bfloat16


def others(axis, n):
    me = lax.axis_index(axis)
    return me, [lax.rem(me + k, n) for k in range(1, n)]


def far_first(ring):
    me = lax.axis_index("seq")
    y, z, core = lax.div(me, 4), lax.div(me, 2) & 1, me & 1
    offsets = [(dy, dz, dc) for dy in range(ring) for dz in range(2) for dc in range(2)]
    offsets.sort(key=lambda o: (-min(o[0], ring - o[0]) - 2 * o[1], o))
    return me, [
        lax.rem(y + dy, ring) * 4 + ((z + dz) & 1) * 2 + ((core + dc) & 1)
        for dy, dz, dc in offsets
        if dy + dz + dc
    ]


def send(src, dst, send_sem, recv_sem, device):
    copy = pltpu.make_async_remote_copy(
        src_ref=src, dst_ref=dst, send_sem=send_sem, recv_sem=recv_sem,
        device_id=device, device_id_type=MESH,
    )
    copy.start()
    return copy


def pieces(x, count):
    out = []
    for k in range(count):
        out.append(x.astype(BF16))
        x = x - out[-1].astype(F32)
    return out


def tile_of(i, j):
    return lax.shift_right_logical(i * (i + 1), 1) + j


def own_start(counts, n):
    me = lax.axis_index("seq")
    start, real = jnp.int32(0), jnp.int32(0)
    for b in range(n):
        start = start + jnp.where(b < me, counts[b], 0)
        real = real + jnp.where(b == me, counts[b], 0)
    return start & (TILE - 1), real


def turn(shift, count):
    row = lax.broadcasted_iota(jnp.int32, (TILE, TILE), 0)
    lane = lax.broadcasted_iota(jnp.int32, (TILE, TILE), 1)
    hit = (lane == ((row + shift) & (TILE - 1))) & (row < count)
    return jnp.where(hit, 1.0, 0.0).astype(BF16)


def enter(x_ref, turned, x_out):
    d = x_out.shape[1]
    for c in range(x_ref.shape[1] // LANES):
        part = lax.dot_general(
            x_ref[:, c * LANES:(c + 1) * LANES], turned, (((0,), (0,)), ((), ())),
            preferred_element_type=F32,
        ).astype(BF16)
        for k in range(LANES // d):
            x_out[c * (LANES // d) + k] = part[k * d:(k + 1) * d]


def pack(starts, spare, x_ref, plain, rows, weights, parts):
    blocks, d, _ = x_ref.shape
    lane = lax.broadcasted_iota(jnp.int32, (d, TILE), 1)
    fill = jnp.zeros((LANES - parts * d, TILE), BF16)
    for c in range(LIVE // TILE):
        v = None
        for b in range(c, min(blocks, c + spare + 1)):
            piece = x_ref[b].astype(F32)
            v = piece if v is None else jnp.where(lane >= starts[b] - c * TILE, piece, v)
        if plain is not None:
            plain[c] = v.astype(BF16)
        rows[c] = jnp.concatenate([v] * (LANES // d), axis=0).T.astype(BF16)
        split = pieces(v * (d ** -0.5 * LOG2E), parts)
        weights[c] = jnp.concatenate(split + [fill] if parts * d < LANES else split, axis=0)


def step(later, now, diagonal, rows, weights, into, source, tops, running, state, keep, other):
    now_at = [tile_of(*c) for c in now]
    now_top = [tops[here] for here in now_at]
    sums = [[jnp.zeros(tops.shape[1:], F32)] * 2 for _ in now]
    made = []
    tallest = [None for _ in later]
    for u in range(max(len(now), len(later))):
        if later:
            i, j = later[u]
            made.append(jnp.dot(rows[j], weights[i], preferred_element_type=F32))
        for g in range(TILE // 8):
            if now:
                v = source[u, g]
                p = jnp.exp2(v - now_top[u])
                sums[u] = [sums[u][0] + p, sums[u][1]]
                if other is None:
                    keep[now_at[u], g] = v
                else:
                    keep[now_at[u], g] = p
                    sums[u][1] = sums[u][1] + p * (v - other[now_at[u], g])
            if later:
                v = made[u][g * 8:(g + 1) * 8]
                if diagonal:
                    row = lax.broadcasted_iota(jnp.int32, v.shape, 0) + g * 8
                    v = jnp.where(row <= lax.broadcasted_iota(jnp.int32, v.shape, 1), v, NEGATIVE)
                into[u, g] = v
                tallest[u] = v if g == 0 else jnp.maximum(tallest[u], v)
    for u, (i, j) in enumerate(later):
        top = jnp.maximum(tallest[u], running[i])
        running[i] = top
        tops[tile_of(i, j)] = top
    for u, (i, _) in enumerate(now):
        less = jnp.exp2(state[i, 0] - now_top[u])
        state[i, 0] = now_top[u]
        state[i, 1] = state[i, 1] * less + sums[u][0]
        if other is not None:
            state[i, 2] = state[i, 2] * less + sums[u][1]


def by_parity(count, even, odd, run):
    @pl.when((count & 1) == 0)
    def _():
        run(even, odd)

    @pl.when((count & 1) == 1)
    def _():
        run(odd, even)


def chain(first, after, count):
    out = [first]
    while len(out) < count:
        out.append(after(*out[-1]))
    return out


def sweep(rows, weights, even, odd, tops, running, state, keep, other):
    blocks = rows.shape[0]
    running[...] = jnp.full(running.shape, NEGATIVE, F32)
    state[:, :1] = jnp.full((blocks, 1, *running.shape[1:]), NEGATIVE, F32)
    state[:, 1:] = jnp.zeros((blocks, state.shape[1] - 1, *running.shape[1:]), F32)

    def run(first, after, tiles, unit, diagonal):
        def one(later, now, into, source):
            step(
                later, now, diagonal, rows, weights, into, source, tops, running, state, keep,
                other,
            )

        def trip(count, now):
            later = chain(after(*now[-1]), after, unit)
            by_parity(count, even, odd, lambda source, into: one(later, now, into, source))
            return later

        now = chain((jnp.int32(first[0]), jnp.int32(first[1])), after, unit)
        one(now, [], even, None)
        trips = tiles // unit - 1
        if trips == 1:
            later = chain(after(*now[-1]), after, unit)
            one(later, now, odd, even)
            now = later
        else:
            now = lax.fori_loop(0, trips, trip, now)
        one([], now, None, odd if trips % 2 else even)

    def below(i, j):
        wrap = j + 1 == i
        return jnp.where(wrap, i + 1, i), jnp.where(wrap, 0, j + 1)

    run((0, 0), lambda i, j: (i + 1, j + 1), blocks, DIAGONAL_TILES, True)
    run((1, 0), below, blocks * (blocks - 1) // 2, LOWER_TILES, False)


def totals(s_state, t_state, stats):
    def collect(state):
        top8 = state[:, 0]
        top = jnp.max(top8, axis=1, keepdims=True)
        less = jnp.exp2(top8 - top)
        return top, [
            jnp.sum(state[:, k] * less, axis=1, keepdims=True) for k in range(1, state.shape[1])
        ]

    s_top, (s_sum,) = collect(s_state)
    t_top, (t_sum, cross) = collect(t_state)
    s_lse = s_top + jnp.log2(s_sum)
    kl = cross / t_sum - (t_top + jnp.log2(t_sum)) + s_lse
    stats[...] = jnp.concatenate([s_lse, t_top, 1.0 / t_sum, s_lse], axis=1)
    return jnp.sum(kl, axis=0) * LN2


def back(i, j):
    wrap = j == i
    return jnp.where(wrap, i - 1, i), jnp.where(wrap, 0, j + 1)


def gradient_step(later, now, into, source, students, s_ref, pt_ref, tops, stats, grad):
    nt = (((1,), (1,)), ((), ()))
    parts = []
    for u in range(max(len(now), len(later))):
        if now:
            i, j = now[u]
            parts.append((
                lax.dot_general(students[i], source[u], nt, preferred_element_type=F32),
                jnp.dot(students[j], source[u], preferred_element_type=F32),
            ))
        if not later:
            continue
        i, j = later[u]
        here = tile_of(i, j)
        s_lse, t_top, t_inv = (stats[i, pl.ds(k, 1), :] for k in range(3))
        t_scale = jnp.exp2(tops[here] - t_top) * t_inv
        for g in range(0, TILE // 8, 2):
            w = jnp.exp2(s_ref[here, g:g + 2] - s_lse) - pt_ref[here, g:g + 2] * t_scale
            into[u, g * 8:g * 8 + 16, :] = w.reshape(16, TILE).astype(BF16)
    for (i, j), (key_grad, query_grad) in zip(now, parts):
        grad[j] += key_grad
        grad[i] += query_grad


def gradients(first, last, final, now, even, odd, row_done, *refs):
    def one(later, now, into, source):
        gradient_step(later, now, into, source, *refs)

    def check(now):
        for i, j in now:
            pl.when(i == j)(functools.partial(row_done, i))

    def trip(count, now):
        later = chain(back(*now[-1]), back, len(now))
        by_parity(count, even, odd, lambda source, into: one(later, now, into, source))
        check(now)
        return later

    now = lax.fori_loop(first, last - final, trip, now)
    if final:
        one([], now, None, odd if (last - 1) % 2 else even)
        check(now)
    return now


def compute_scratch(dt, ds):
    blocks = LIVE // TILE
    tiles = blocks * (blocks + 1) // 2
    groups = TILE // 8
    wide = max(DIAGONAL_TILES, LOWER_TILES)
    return dict(
        students=pltpu.VMEM((blocks, ds, TILE), BF16),
        rows=pltpu.VMEM((2, blocks, TILE, LANES), BF16),
        weights=pltpu.VMEM((2, blocks, LANES, TILE), BF16),
        even=pltpu.VMEM((wide, groups, 8, TILE), F32),
        odd=pltpu.VMEM((wide, groups, 8, TILE), F32),
        s_ref=pltpu.VMEM((tiles, groups, 8, TILE), F32),
        pt_ref=pltpu.VMEM((tiles, groups, 8, TILE), F32),
        tops=pltpu.VMEM((tiles, 8, TILE), F32),
        running=pltpu.VMEM((blocks, 8, TILE), F32),
        s_state=pltpu.VMEM((blocks, 2, 8, TILE), F32),
        t_state=pltpu.VMEM((blocks, 3, 8, TILE), F32),
        stats=pltpu.VMEM((blocks, 4, TILE), F32),
        w_even=pltpu.VMEM((GRADIENT_TILES, TILE, TILE), BF16),
        w_odd=pltpu.VMEM((GRADIENT_TILES, TILE, TILE), BF16),
        grad=pltpu.VMEM((blocks, ds, TILE), F32),
    )


def student_phase(starts, spare, x_in, c):
    pack(starts, spare, x_in, c["students"], c["rows"].at[0], c["weights"].at[0], 3)
    sweep(
        c["rows"].at[0], c["weights"].at[0], c["even"], c["odd"], c["tops"],
        c["running"], c["s_state"], c["s_ref"], None,
    )


def teacher_phase(starts, spare, x_in, c):
    pack(starts, spare, x_in, None, c["rows"].at[1], c["weights"].at[1], 2)
    sweep(
        c["rows"].at[1], c["weights"].at[1], c["even"], c["odd"], c["tops"],
        c["running"], c["t_state"], c["pt_ref"], c["s_ref"],
    )
    return totals(c["s_state"], c["t_state"], c["stats"])


def gradient_phase(first, last, final, now, c, row_done):
    refs = [c[k] for k in ("students", "s_ref", "pt_ref", "tops", "stats", "grad")]
    if now is None:
        now = chain((jnp.int32(LIVE // TILE - 1), jnp.int32(0)), back, GRADIENT_TILES)
        gradient_step(now, [], c["w_even"], None, *refs)
    return gradients(first, last, final, now, c["w_even"], c["w_odd"], row_done, *refs)


def kernel(
    n, m, counts, t_ref, s_ref, g_in, loss_ref,
    t_own, s_own, t_out, s_out, t_in, s_in, c, g_out, starts, part, row, grid, sems,
):
    x_send, x_recv, g_send, g_recv, seq_send, seq_recv, head_send, head_recv, own = sems
    blocks = LIVE // TILE
    spare = n - blocks
    grad = c["grad"]
    ds = grad.shape[1]
    me, peers = far_first(n // 4)
    my_head, head_peers = others("head", m)
    barrier = pltpu.get_barrier_semaphore()
    for peer in [{"seq": p} for p in peers] + [{"head": p} for p in head_peers]:
        pl.semaphore_signal(barrier, inc=1, device_id=peer, device_id_type=MESH)

    s_load = pltpu.make_async_copy(s_ref, s_own, own.at[0])
    t_load = pltpu.make_async_copy(t_ref, t_own, own.at[1])
    s_load.start()
    t_load.start()
    shift, _ = own_start(counts, n)
    turned = turn(shift, TILE)
    s_load.wait()
    enter(s_own, turned, s_out)
    start = jnp.int32(0)
    scalars = []
    for b in range(n):
        starts[b] = start
        scalars.append(start)
        start = start + counts[b]
    grad[...] = jnp.zeros_like(grad)
    pl.semaphore_wait(barrier, n - 1 + m - 1)

    copies, keeps = [], []
    for kind, (src, dst) in enumerate(((s_out, s_in), (t_out, t_in))):
        if kind:
            t_load.wait()
            enter(t_own, turned, t_out)
        for copy in copies[0] if kind else []:
            copy.wait_send()
        keeps.append(pltpu.make_async_copy(src.at[me], dst.at[me], own.at[kind]))
        keeps[kind].start()
        copies.append([
            send(src.at[p], dst.at[me], x_send.at[kind, k], x_recv.at[kind, k], {"seq": p})
            for k, p in enumerate(peers)
        ])
    keeps[0].wait()
    for copy in copies[0]:
        copy.wait_recv()
    student_phase(scalars, spare, s_in, c)
    keeps[1].wait()
    for copy in copies[1]:
        copy.wait()
    loss = teacher_phase(scalars, spare, t_in, c)
    part[...] = loss[:, :LANES] + loss[:, LANES:]

    def finish_block(b):
        lane = lax.broadcasted_iota(jnp.int32, grad.shape[1:], 1)
        first = starts[b]
        top = blocks - 1
        v = grad[jnp.minimum(b, top)]
        for k in range(1, spare + 1):
            q = jnp.clip(b - k, 0, top)
            v = jnp.where(lane + q * TILE >= first, grad[q], v)
        g_out[b] = v.astype(BF16)

    def to_owner(b):
        @pl.when(b == me)
        def _():
            pltpu.make_async_copy(g_out.at[b], g_in.at[me], own.at[1]).start()

        @pl.when(b != me)
        def _():
            send(g_out.at[b], g_in.at[me], g_send.at[b], g_recv.at[me], {"seq": b})

    def row_done(i):
        @pl.when(i + spare + 1 < n)
        def _():
            to_owner(i + spare + 1)

        finish_block(i + spare)

    trips = blocks * (blocks + 1) // 2 // GRADIENT_TILES
    now = gradient_phase(0, 0, False, None, c, row_done)
    own_part = pltpu.make_async_copy(part, row.at[me], own.at[0])
    own_part.start()
    parts = [
        send(part, row.at[me], seq_send.at[k], seq_recv.at[k], {"seq": p})
        for k, p in enumerate(peers)
    ]
    now = gradient_phase(0, trips - 1, False, now, c, row_done)
    own_part.wait()
    for copy in parts:
        copy.wait()
    own_row = pltpu.make_async_copy(row, grid.at[my_head], own.at[0])
    own_row.start()
    row_copies = [
        send(row, grid.at[my_head], head_send.at[k], head_recv.at[k], {"head": p})
        for k, p in enumerate(head_peers)
    ]
    gradient_phase(trips - 1, trips, True, now, c, row_done)
    for b in range(spare):
        finish_block(b)
    for b in range(spare, -1, -1):
        to_owner(b)
    own_row.wait()
    for copy in row_copies:
        copy.wait()
    whole = jnp.int32(0)
    for b in range(n):
        whole = whole + counts[b]
    loss_ref[...] = jnp.sum(jnp.sum(grid[...], axis=(0, 1)), axis=1, keepdims=True) / (
        H_REL * whole.astype(F32)
    )
    pltpu.make_async_copy(g_out.at[me], g_in.at[me], own.at[1]).wait()
    for p in peers:
        pltpu.make_async_remote_copy(
            src_ref=g_out.at[p], dst_ref=g_in.at[p], send_sem=g_send.at[p],
            recv_sem=g_recv.at[p], device_id={"seq": p}, device_id_type=MESH,
        ).wait()


def leave_kernel(n, counts, g_ref, o_ref):
    ds = g_ref.shape[1]
    per = TILE // ds
    turned = turn(*own_start(counts, n))
    for k in range(n // per):
        o_ref[:, k * TILE:(k + 1) * TILE] = ds ** -0.5 * lax.dot_general(
            turned, g_ref[k * per:(k + 1) * per].reshape(TILE, TILE),
            (((1,), (1,)), ((), ())), preferred_element_type=F32,
        )


def local(teacher, student, counts):
    n, m = lax.axis_size("seq"), lax.axis_size("head")
    tokens = teacher.shape[0]
    dt, ds = teacher.shape[1] // n, student.shape[1] // n
    vmem = pl.BlockSpec(memory_space=pltpu.VMEM)
    any_space = pl.BlockSpec(memory_space=pl.ANY)
    smem = pl.BlockSpec(memory_space=pltpu.SMEM)
    dma = pltpu.SemaphoreType.DMA
    grad, loss = pl.pallas_call(
        functools.partial(kernel, n, m),
        out_shape=(
            jax.ShapeDtypeStruct((n, ds, tokens), BF16),
            jax.ShapeDtypeStruct((1, 1), F32),
        ),
        in_specs=[smem, any_space, any_space],
        out_specs=(any_space, vmem),
        scratch_shapes=[
            pltpu.VMEM(teacher.shape, BF16),
            pltpu.VMEM(student.shape, BF16),
            pltpu.VMEM((n, dt, tokens), BF16),
            pltpu.VMEM((n, ds, tokens), BF16),
            pltpu.VMEM((n, dt, tokens), BF16),
            pltpu.VMEM((n, ds, tokens), BF16),
            compute_scratch(dt, ds),
            pltpu.VMEM((n, ds, tokens), BF16),
            pltpu.SMEM((n,), jnp.int32),
            pltpu.VMEM((1, LANES), F32),
            pltpu.VMEM((n, 1, LANES), F32),
            pltpu.VMEM((m, n, 1, LANES), F32),
            [dma((2, n - 1))] * 2 + [dma((n,))] * 2 + [dma((n - 1,))] * 2
            + [dma((m - 1,))] * 2 + [dma((2,))],
        ],
        compiler_params=pltpu.CompilerParams(
            collective_id=0, has_side_effects=True, vmem_limit_bytes=62 << 20
        ),
    )(counts, teacher, student)
    grad = pl.pallas_call(
        functools.partial(leave_kernel, n),
        out_shape=jax.ShapeDtypeStruct((tokens, n * ds), F32),
        in_specs=[smem, vmem],
        out_specs=vmem,
    )(counts, grad)
    return grad, loss.reshape(())


def solution(mesh):
    return jax.shard_map(
        local,
        mesh=mesh,
        in_specs=(P("seq", "head"), P("seq", "head"), P()),
        out_specs=(P("seq", "head"), P()),
        check_vma=False,
    )
```
